256 devices in a mesh: track: 8 (over x, core), tile: 32 (over z, y).
Axes of the slice: x: 4, y: 4, z: 8, core: 2. Of those that a mesh axis runs over, the one named last changes fastest.
Arguments:
- panels: bfloat16 [262144, 1024], P(('track', 'tile')), may hold values from -6 to 6
- phases: float32 [16384], P(('track', 'tile')), may hold values from -3.140625 to 3.140625
- weight_tiles: bfloat16 [4, 1024, 512], replicated, may hold values from -0.015625 to 0.015625
- tile_class: int32 [1024], P(('track', 'tile')), may hold values from 0 to 3
- send_slots: int32 [196608], P(('track', 'tile')), may hold values from -1 to 1023, as said below
- foot_slot: int32 [1024, 512], P(('track', 'tile')), may hold values from 0 to 767, as said below
- foot_ping: int32 [1024, 512], P(('track', 'tile')), may hold values from 0 to 16383, as said below
- tile_counts: int32 [1024], P(('track', 'tile')), may hold values from 102 to 512, as said below
Outputs:
- image: float32 [1024, 2, 1024], P(('track', 'tile'))
- ping_gradient: float32 [16384], P(('track', 'tile'))
The draws below stay inside these ranges and needn't reach their ends.
Inputs may be any that keep to these rules, and one draw needn't show every extreme that they name: `send_slots`: entries name local panel rows of the sending device; an entry is -1 exactly where the track group of its offset (offset minus 1) lies outside the slice. `foot_slot`: the entries of one tile are distinct slots, each of which holds a panel. foot_ping[t, f] is the ping of the panel in slot foot_slot[t, f] of tile t's device. `tile_counts`: only the first tile_counts_t entries of tile t's footprint lists are used.
All inputs are finite; a program needn't handle non-finite values.
Results may differ from the reference program's by a relative error of at most 0.0065.
Values may be sent and summed in bfloat16 or wider, within the bound.
No kernel may reach another device: no remote copies, remote signals or barrier semaphores. Data moves between devices by JAX's collectives and lax.ppermute only.
A program may use at most 128 MiB of HBM per device.

```python
import jax
import jax.numpy as jnp
from jax import lax

BINS = 512
RBLK = 16
TPIX = 1024
NWT = 4
TILES_DEV = 4
FOOT = 512
BLK = 128
GROUP = 256
PING_DEV = 64
CAP = 8
PINGS = 16384
TILES = 1024
N_TRACK = 8
N_TILE = 32


def routing_tables(key):
    key_send, key_rank = jax.random.split(jax.random.fold_in(key, 11))
    rows_dev = PING_DEV * RBLK
    send_shape = (N_TRACK, N_TILE, 3, N_TILE, CAP)
    sent = jax.random.randint(key_send, send_shape, 0, rows_dev, dtype=jnp.int32)
    sender_track = lax.broadcasted_iota(jnp.int32, send_shape, 0)
    send_offset = lax.broadcasted_iota(jnp.int32, send_shape, 2)
    target_track = sender_track + send_offset - 1
    sent = jnp.where((target_track >= 0) & (target_track < N_TRACK), sent, -1)
    recv_shape = (N_TRACK, N_TILE, TILES_DEV, 3, N_TILE, CAP)
    recv_track = lax.broadcasted_iota(jnp.int32, recv_shape, 0)
    recv_offset = lax.broadcasted_iota(jnp.int32, recv_shape, 3)
    recv_source = lax.broadcasted_iota(jnp.int32, recv_shape, 4)
    recv_slot = lax.broadcasted_iota(jnp.int32, recv_shape, 5)
    from_track = recv_track + recv_offset - 1
    inside = (from_track >= 0) & (from_track < N_TRACK)
    flat_pos = (recv_offset * N_TILE + recv_source) * CAP + recv_slot
    scores = jax.random.randint(key_rank, recv_shape, 0, 1 << 20, dtype=jnp.int32)
    sort_keys = jnp.where(inside, scores * (3 * GROUP) + flat_pos, (1 << 30) + flat_pos)
    sort_keys = sort_keys.reshape(N_TRACK * N_TILE * TILES_DEV, 3 * GROUP)
    ranking = jnp.argsort(sort_keys, axis=1, stable=True)[:, :FOOT].astype(jnp.int32)
    row_device = jnp.arange(N_TRACK * N_TILE * TILES_DEV, dtype=jnp.int32)[:, None] // TILES_DEV
    own_track = row_device // N_TILE
    own_tile = row_device % N_TILE
    offset = ranking // GROUP
    source_tile = ranking // CAP % N_TILE
    slot_pos = ranking % CAP
    source_track = jnp.clip(own_track + offset - 1, 0, N_TRACK - 1)
    local_row = sent[source_track, source_tile, 2 - offset, own_tile, slot_pos]
    pings = (source_track * N_TILE + source_tile) * PING_DEV + jnp.maximum(local_row, 0) // RBLK
    return (sent.reshape(-1), ranking, pings.astype(jnp.int32))


def draw_send_slots(key, part):
    return routing_tables(key)[0]


def draw_foot_slot(key, part):
    return routing_tables(key)[1]


def draw_foot_ping(key, part):
    return routing_tables(key)[2]


def draw_tile_counts(key, part):
    key_div, key_pick = jax.random.split(jax.random.fold_in(key, 5))
    total = N_TRACK * N_TILE * TILES_DEV
    divisor = jax.random.randint(key_div, (total,), 1, 6, dtype=jnp.int32)
    counts = FOOT // divisor
    chosen = jax.random.randint(key_pick, (), 0, total, dtype=jnp.int32)
    return jnp.where(jnp.arange(total, dtype=jnp.int32) == chosen, FOOT, counts).astype(jnp.int32)


def with_ends(values, own_key, least, top_value):
    dims = values.shape
    index_at = [jax.random.randint(jax.random.fold_in(own_key, axis), (), 0, dims[axis]) for axis in range(len(dims))]
    values = values.at[tuple(index_at)].set(least)
    longest = dims.index(max(dims))
    index_at[longest] = (index_at[longest] + 1) % dims[longest]
    return values.at[tuple(index_at)].set(top_value)


def level_of(rng, extent, pieces, smallest, top_value):
    factor_of = 1.0
    for dim, parts in pieces:
        heights = jax.random.uniform(jax.random.fold_in(jax.random.fold_in(rng, 6), dim), (parts,), jnp.float32, smallest / len(pieces), top_value / len(pieces))
        factor_of = factor_of * jnp.repeat(jnp.exp(heights), extent[dim] // parts).reshape((-1,) + (1,) * (len(extent) - 1 - dim))
    return factor_of


def gaussian(key, dims, spread, limit, cuts=(), kind=jnp.bfloat16):
    array = jax.random.normal(key, dims, jnp.float32) * spread
    if len(cuts) > 0:
        array = level_of(key, dims, cuts, -0.22, 0.18) * array
    return jnp.clip(array, min=-limit, max=limit).astype(kind)


def setup_inputs(seed: int = 0) -> dict:
    key_of = jax.random.split(jax.random.key(seed), 9)
    return {
        "panels": gaussian(key_of[0], (PINGS * RBLK, 2 * BINS), 1.0, 6.0, ((0, 256),)),
        "phases": jnp.clip(jax.random.uniform(key_of[1], (PINGS,), jnp.float32, -3.140625, 3.140625), -3.140625, 3.140625),
        "weight_tiles": gaussian(key_of[2], (NWT, TPIX, BINS), (BINS * FOOT // 2) ** -0.5, 0.015625),
        "tile_class": with_ends(jax.random.randint(key_of[3], (TILES,), 0, NWT), jax.random.fold_in(key_of[3], 1), 0, NWT - 1).astype(jnp.int32),
        "send_slots": draw_send_slots(jax.random.fold_in(key_of[8], 71), 0),
        "foot_slot": draw_foot_slot(jax.random.fold_in(key_of[8], 71), 0),
        "foot_ping": draw_foot_ping(jax.random.fold_in(key_of[8], 71), 0),
        "tile_counts": draw_tile_counts(jax.random.fold_in(key_of[8], 71), 0),
    }


def rotate_panels(panels, phases):
    bin_count = panels.shape[1] // 2
    blocks_per_ping = panels.shape[0] // phases.shape[0]
    cos_rows = jnp.repeat(jnp.cos(phases), blocks_per_ping)[:, None]
    sin_rows = jnp.repeat(jnp.sin(phases), blocks_per_ping)[:, None]
    real_part = panels[:, :bin_count].astype(jnp.float32)
    imag_part = panels[:, bin_count:].astype(jnp.float32)
    turned = jnp.concatenate([cos_rows * real_part - sin_rows * imag_part, sin_rows * real_part + cos_rows * imag_part], axis=1)
    return turned.astype(jnp.bfloat16)


def phase_terms(ping_ids, tile_global, ping_total, tile_total, track_groups, pixels):
    offset = (2 * ping_ids + 1) * tile_total - (2 * tile_global + 1) * ping_total
    along = offset.astype(jnp.float32) * (track_groups / (2.0 * ping_total * tile_total))
    across = (jnp.arange(pixels, dtype=jnp.int32).astype(jnp.float32) + 0.5) / pixels - 0.5
    angles = 96.0 * across[:, None] * along[None, :] + 8.0 * (along * along)[None, :]
    return jnp.cos(angles), jnp.sin(angles)


def reference(panels, phases, weight_tiles, tile_class, send_slots, foot_slot, foot_ping, tile_counts):
    rows_dev = PING_DEV * RBLK
    rotated = rotate_panels(panels, phases)
    table = send_slots.reshape(N_TRACK, N_TILE, 3, N_TILE, CAP)
    track_ids = jnp.arange(N_TRACK, dtype=jnp.int32)[:, None, None, None, None]
    tile_ids = jnp.arange(N_TILE, dtype=jnp.int32)[None, :, None, None, None]
    offsets = jnp.arange(3, dtype=jnp.int32)[None, None, :, None, None]
    source_tile = jnp.arange(N_TILE, dtype=jnp.int32)[None, None, None, :, None]
    slot_pos = jnp.arange(CAP, dtype=jnp.int32)[None, None, None, None, :]
    source_track = track_ids + offsets - 1
    inside = (source_track >= 0) & (source_track < N_TRACK)
    clipped = jnp.clip(source_track, 0, N_TRACK - 1)
    local_row = table[clipped, source_tile, 2 - offsets, tile_ids, slot_pos]
    global_row = jnp.where(inside & (local_row >= 0), (clipped * N_TILE + source_tile) * rows_dev + local_row, -1)
    global_row = global_row.reshape(N_TRACK * N_TILE, 3 * GROUP)
    owner = jnp.arange(TILES, dtype=jnp.int32) // TILES_DEV
    entry_rows = global_row[owner[:, None], foot_slot]

    def one_tile(inputs):
        tile_global, row_ids, ping_ids, entry_count, weight_class = inputs
        weight = weight_tiles[weight_class]
        present = row_ids >= 0
        data = jnp.where(present[:, None], rotated[jnp.maximum(row_ids, 0)], jnp.zeros((), jnp.bfloat16))
        block_count = (entry_count + BLK - 1) // BLK
        positions = jnp.arange(BLK, dtype=jnp.int32)

        def block_terms(block):
            start = (block * BLK).astype(jnp.int32)
            rows = lax.dynamic_slice_in_dim(data, start, BLK, 0)
            block_pings = lax.dynamic_slice_in_dim(ping_ids, start, BLK, 0)
            cos_grid, sin_grid = phase_terms(block_pings, tile_global, PINGS, TILES, N_TRACK, TPIX)
            active = (start + positions < entry_count).astype(jnp.float32)
            real_proj = jnp.dot(weight, rows[:, :BINS].T, preferred_element_type=jnp.float32)
            imag_proj = jnp.dot(weight, rows[:, BINS:].T, preferred_element_type=jnp.float32)
            return real_proj, imag_proj, cos_grid, sin_grid, active, start

        def forward_step(block, carry):
            real_sum, imag_sum = carry
            real_proj, imag_proj, cos_grid, sin_grid, active, start = block_terms(block)
            real_sum = real_sum + jnp.sum((cos_grid * real_proj - sin_grid * imag_proj) * active[None, :], axis=1)
            imag_sum = imag_sum + jnp.sum((sin_grid * real_proj + cos_grid * imag_proj) * active[None, :], axis=1)
            return real_sum, imag_sum

        zero_row = jnp.zeros((TPIX,), jnp.float32)
        real_sum, imag_sum = lax.fori_loop(0, block_count, forward_step, (zero_row, zero_row))
        intensity = real_sum * real_sum + imag_sum * imag_sum
        heavy_real = intensity * real_sum
        heavy_imag = intensity * imag_sum

        def adjoint_step(block, values):
            real_proj, imag_proj, cos_grid, sin_grid, active, start = block_terms(block)
            adj_real = (heavy_imag[:, None] * cos_grid - heavy_real[:, None] * sin_grid).astype(jnp.bfloat16)
            adj_imag = (-(heavy_imag[:, None] * sin_grid + heavy_real[:, None] * cos_grid)).astype(jnp.bfloat16)
            correlation = jnp.sum(real_proj * adj_real.astype(jnp.float32) + imag_proj * adj_imag.astype(jnp.float32), axis=0)
            return lax.dynamic_update_slice_in_dim(values, correlation * active, start, 0)

        values = lax.fori_loop(0, block_count, adjoint_step, jnp.zeros((FOOT,), jnp.float32))
        return jnp.stack([real_sum, imag_sum]), values

    tile_index = jnp.arange(TILES, dtype=jnp.int32)
    images, values = lax.map(one_tile, (tile_index, entry_rows, foot_ping, tile_counts, tile_class))
    ping_of = jnp.maximum(entry_rows, 0) // RBLK
    gradient = jax.ops.segment_sum(values.reshape(-1), ping_of.reshape(-1), num_segments=PINGS)
    return images, gradient
```

```python
import jax
import jax.numpy as jnp
from jax import lax
from jax.experimental import pallas as pl
from jax.experimental.pallas import tpu as pltpu
from jax.sharding import PartitionSpec as P

LANES = 128
HALF = 128
VMEM_BYTES = 56 * 1024 * 1024


def shift_along(block, axis, distance):
    devices = range(lax.axis_size(axis))
    route = [(i - distance, i) for i in devices if i - distance in devices]
    return lax.ppermute(block, axis, route)


def whole(shape):
    return pl.BlockSpec(shape, lambda *_: (0,) * len(shape))


def column(row):
    return jnp.broadcast_to(row, (8, row.shape[1])).T[:, :1]


def gather_kernel(panels_ref, phases_ref, slots_ref, out_ref):
    rows_here, width = panels_ref.shape
    bins = width // 2
    pings = phases_ref.shape[1]
    count = out_ref.shape[0]
    slot_row = column(slots_ref[0].astype(jnp.float32)).astype(jnp.int32)
    row_ids = lax.broadcasted_iota(jnp.int32, (count, rows_here), 1)
    pick = jnp.where(row_ids == slot_row, 1.0, 0.0).astype(jnp.bfloat16)
    picked = jnp.dot(pick, panels_ref[...], preferred_element_type=jnp.float32)
    phases = phases_ref[...]
    ping_ids = lax.broadcasted_iota(jnp.int32, (count, pings), 1)
    owned = ping_ids == (slot_row // (rows_here // pings))
    cos_col = jnp.sum(jnp.where(owned, jnp.cos(phases), 0.0), axis=1, keepdims=True)
    sin_col = jnp.sum(jnp.where(owned, jnp.sin(phases), 0.0), axis=1, keepdims=True)
    real_part = picked[:, :bins]
    imag_part = picked[:, bins:]
    out_ref[:, :bins] = (cos_col * real_part - sin_col * imag_part).astype(jnp.bfloat16)
    out_ref[:, bins:] = (sin_col * real_part + cos_col * imag_part).astype(jnp.bfloat16)


def gather_rotated(panels, phases, slots, steps):
    total = slots.shape[0]
    count = total // steps
    return pl.pallas_call(
        gather_kernel,
        grid=(steps,),
        in_specs=[
            whole(panels.shape),
            whole((1, phases.shape[0])),
            pl.BlockSpec((1, 1, count), lambda i: (i, 0, 0)),
        ],
        out_specs=pl.BlockSpec((count, panels.shape[1]), lambda i: (i, 0)),
        out_shape=jax.ShapeDtypeStruct((total, panels.shape[1]), jnp.bfloat16),
        compiler_params=pltpu.CompilerParams(vmem_limit_bytes=VMEM_BYTES),
        name="gather_rotated",
    )(panels, phases.reshape(1, -1), slots.reshape(steps, 1, count))


def make_table_kernel(ping_total, tile_total, track_groups, pixels, tiles_here, slots):
    def table_kernel(base_ref, counts_ref, slot_ref, ping_ref, base_cos, base_sin, step_cos, step_sin):
        tile = pl.program_id(0)
        foot = slot_ref.shape[2]
        count = counts_ref[tile]
        tile_global = base_ref[0] + tile
        slot_ids = lax.broadcasted_iota(jnp.int32, (slots, foot), 0)
        match = jnp.where(slot_ids == slot_ref[0], 1.0, 0.0).astype(jnp.bfloat16)
        pings = ping_ref[0]
        used = jnp.where(lax.broadcasted_iota(jnp.int32, (1, foot), 1) < count, 1.0, 0.0)
        values = jnp.concatenate(
            [
                (pings // HALF).astype(jnp.float32) * used,
                (pings % HALF).astype(jnp.float32) * used,
                used,
                jnp.zeros((5, foot), jnp.float32),
            ],
            axis=0,
        ).astype(jnp.bfloat16)
        found = lax.dot_general(
            match, values, (((1,), (1,)), ((), ())), preferred_element_type=jnp.float32
        )
        ping = (found[:, 0:1] * HALF + found[:, 1:2]).astype(jnp.int32)
        mask = found[:, 2:3]
        offset = (2 * ping + 1) * tile_total - (2 * tile_global + 1) * ping_total
        along = offset.astype(jnp.float32) * (track_groups / (2.0 * ping_total * tile_total))
        lane = lax.broadcasted_iota(jnp.int32, (1, LANES), 1).astype(jnp.float32)
        across = (lane + 0.5) / pixels - 0.5
        angle = 96.0 * across * along + 8.0 * (along * along)
        base_cos[0] = jnp.cos(angle) * mask
        base_sin[0] = jnp.sin(angle) * mask
        step = jnp.broadcast_to((96.0 * LANES / pixels) * along, (slots, 8))
        step_cos[0] = jnp.broadcast_to(jnp.cos(step)[:, :1], (slots, LANES))
        step_sin[0] = jnp.broadcast_to(jnp.sin(step)[:, :1], (slots, LANES))

    return table_kernel


def phase_tables(base, counts, foot_slot, foot_ping, slots, ping_total, tile_total, track_groups, pixels):
    tiles_here, foot = foot_slot.shape
    kernel = make_table_kernel(ping_total, tile_total, track_groups, pixels, tiles_here, slots)
    table = jax.ShapeDtypeStruct((tiles_here, slots, LANES), jnp.float32)
    return pl.pallas_call(
        kernel,
        grid_spec=pltpu.PrefetchScalarGridSpec(
            num_scalar_prefetch=2,
            grid=(tiles_here,),
            in_specs=[pl.BlockSpec((1, 1, foot), lambda t, *_: (t, 0, 0))] * 2,
            out_specs=[pl.BlockSpec((1, slots, LANES), lambda t, *_: (t, 0, 0))] * 4,
        ),
        out_shape=[table] * 4,
        compiler_params=pltpu.CompilerParams(vmem_limit_bytes=VMEM_BYTES),
        name="phase_tables",
    )(base, counts, foot_slot.reshape(tiles_here, 1, foot), foot_ping.reshape(tiles_here, 1, foot))


def make_focus_kernel(slots, pixels, bins, chunk):
    blocks = pixels // LANES

    def focus_kernel(
        class_ref, rows_ref, weight_ref, base_cos, base_sin, step_cos, step_sin,
        image_ref, corr_ref, proj_r, proj_i, turned_r, turned_i, corr_acc,
    ):
        tile = pl.program_id(0)
        weight = weight_ref[0]
        sums = None
        for start in range(0, slots, chunk):
            half = (start // chunk) % 2
            rows = rows_ref[pl.ds(start, chunk), :]
            dims = (((1,), (1,)), ((), ()))
            proj_r[half] = lax.dot_general(rows[:, :bins], weight, dims, preferred_element_type=jnp.float32)
            proj_i[half] = lax.dot_general(rows[:, bins:], weight, dims, preferred_element_type=jnp.float32)

            def group(i, carry, start=start, half=half):
                at = pl.multiple_of(start + i * 8, 8)
                local = pl.multiple_of(i * 8, 8)
                cos_now = base_cos[0, pl.ds(at, 8), :]
                sin_now = base_sin[0, pl.ds(at, 8), :]
                turn_c = step_cos[0, pl.ds(at, 8), :]
                turn_s = step_sin[0, pl.ds(at, 8), :]
                out = []
                for b in range(blocks):
                    lanes = pl.ds(b * LANES, LANES)
                    real = proj_r[half, pl.ds(local, 8), lanes]
                    imag = proj_i[half, pl.ds(local, 8), lanes]
                    new_r = cos_now * real - sin_now * imag
                    new_i = sin_now * real + cos_now * imag
                    turned_r[pl.ds(at, 8), lanes] = new_r
                    turned_i[pl.ds(at, 8), lanes] = new_i
                    out.append(carry[2 * b] + new_r)
                    out.append(carry[2 * b + 1] + new_i)
                    if b + 1 < blocks:
                        cos_now, sin_now = (
                            cos_now * turn_c - sin_now * turn_s,
                            sin_now * turn_c + cos_now * turn_s,
                        )
                return tuple(out)

            if sums is None:
                sums = (jnp.zeros((8, LANES), jnp.float32),) * (2 * blocks)
            sums = lax.fori_loop(0, chunk // 8, group, sums, unroll=2)
        heavy = []
        for b in range(blocks):
            lanes = pl.ds(b * LANES, LANES)
            real = jnp.sum(sums[2 * b], axis=0, keepdims=True)
            imag = jnp.sum(sums[2 * b + 1], axis=0, keepdims=True)
            image_ref[0, 0:1, lanes] = real
            image_ref[0, 1:2, lanes] = imag
            intensity = real * real + imag * imag
            heavy.append(jnp.broadcast_to(intensity * real, (8, LANES)))
            heavy.append(jnp.broadcast_to(intensity * imag, (8, LANES)))

        @pl.when(tile == 0)
        def _():
            corr_acc[...] = jnp.zeros_like(corr_acc)

        def pull(i, _):
            at = pl.multiple_of(i * 8, 8)
            total = corr_acc[pl.ds(at, 8), :]
            for b in range(blocks):
                lanes = pl.ds(b * LANES, LANES)
                total = total + (
                    turned_r[pl.ds(at, 8), lanes] * heavy[2 * b + 1]
                    - turned_i[pl.ds(at, 8), lanes] * heavy[2 * b]
                )
            corr_acc[pl.ds(at, 8), :] = total
            return 0

        lax.fori_loop(0, slots // 8, pull, 0, unroll=2)

        @pl.when(tile == pl.num_programs(0) - 1)
        def _():
            for part in range(slots // LANES):
                block = corr_acc[pl.ds(part * LANES, LANES), :]
                corr_ref[pl.ds(part, 1), :] = jnp.sum(block.T, axis=0, keepdims=True)

    return focus_kernel


def focus(tile_class, received, weight_tiles, tables, chunk):
    slots, width = received.shape
    _, pixels, bins = weight_tiles.shape
    tiles_here = tile_class.shape[0]
    parts = slots // LANES
    table_spec = pl.BlockSpec((1, slots, LANES), lambda t, *_: (t, 0, 0))
    image, corr = pl.pallas_call(
        make_focus_kernel(slots, pixels, bins, chunk),
        grid_spec=pltpu.PrefetchScalarGridSpec(
            num_scalar_prefetch=1,
            grid=(tiles_here,),
            in_specs=[
                whole((slots, width)),
                pl.BlockSpec((1, pixels, bins), lambda t, cls: (cls[t], 0, 0)),
            ]
            + [table_spec] * 4,
            out_specs=[
                pl.BlockSpec((1, 2, pixels), lambda t, *_: (t, 0, 0)),
                whole((parts, LANES)),
            ],
            scratch_shapes=[
                pltpu.VMEM((2, chunk, pixels), jnp.float32),
                pltpu.VMEM((2, chunk, pixels), jnp.float32),
                pltpu.VMEM((slots, pixels), jnp.float32),
                pltpu.VMEM((slots, pixels), jnp.float32),
                pltpu.VMEM((slots, LANES), jnp.float32),
            ],
        ),
        out_shape=[
            jax.ShapeDtypeStruct((tiles_here, 2, pixels), jnp.float32),
            jax.ShapeDtypeStruct((parts, LANES), jnp.float32),
        ],
        compiler_params=pltpu.CompilerParams(
            dimension_semantics=("arbitrary",), vmem_limit_bytes=VMEM_BYTES
        ),
        name="focus",
    )(tile_class, received, weight_tiles, *tables)
    return image, corr.reshape(slots)


def on_device(
    panels, phases, weight_tiles, tile_class, send_slots, foot_slot, foot_ping, tile_counts
):
    track_devs = lax.axis_size("track")
    tile_devs = lax.axis_size("tile")
    device = lax.axis_index("track") * tile_devs + lax.axis_index("tile")
    ping_local = phases.shape[0]
    row_width = panels.shape[1]
    tiles_here = tile_counts.shape[0]
    pixels = weight_tiles.shape[1]
    slots = send_slots.shape[0]
    slot_cap = slots // 3 // tile_devs
    ping_total = ping_local * track_devs * tile_devs
    tile_total = tiles_here * track_devs * tile_devs

    outgoing = gather_rotated(panels, phases, send_slots, 3)
    outgoing = outgoing.reshape(3, tile_devs, slot_cap, row_width)
    behind = shift_along(outgoing[2], "track", 1)
    ahead = shift_along(outgoing[0], "track", -1)
    mixed = jnp.concatenate([behind, outgoing[1], ahead], axis=1)
    arrived = lax.all_to_all(mixed, "tile", split_axis=0, concat_axis=0, tiled=True)
    tables = phase_tables(
        (device * tiles_here).astype(jnp.int32).reshape(1),
        tile_counts, foot_slot, foot_ping, slots,
        ping_total, tile_total, track_devs, pixels,
    )
    received = arrived.reshape(tile_devs, 3, slot_cap, row_width).transpose(1, 0, 2, 3)
    image, corr = focus(tile_class, received.reshape(slots, row_width), weight_tiles, tables, 128)

    partial = corr.reshape(3, tile_devs, slot_cap)
    behind = shift_along(partial[2], "track", 1)
    ahead = shift_along(partial[0], "track", -1)
    back = jnp.concatenate([behind, partial[1], ahead], axis=1)
    back = lax.all_to_all(back, "tile", split_axis=0, concat_axis=0, tiled=True)
    back = back.reshape(tile_devs, 3, slot_cap).transpose(1, 0, 2).reshape(1, slots)
    owner = (send_slots // (panels.shape[0] // ping_local)).reshape(1, slots)
    own = lax.broadcasted_iota(jnp.int32, (ping_local, slots), 0) == owner
    ping_gradient = jnp.sum(jnp.where(own & (send_slots >= 0)[None, :], back, 0.0), axis=1)
    return (image, ping_gradient)


def solution(mesh):
    spread = P(("track", "tile"))
    in_specs = (
        P(("track", "tile"), None), spread, P(), spread, spread,
        P(("track", "tile"), None), P(("track", "tile"), None), spread,
    )
    out_specs = (P(("track", "tile"), None, None), spread)
    return jax.shard_map(
        on_device, mesh=mesh, in_specs=in_specs, out_specs=out_specs, check_vma=False
    )
```

```python
import jax
import jax.numpy as jnp
from jax import lax
from jax.experimental import pallas as pl
from jax.experimental.pallas import tpu as pltpu
from jax.sharding import PartitionSpec as P

LANES = 128
HALF = 128
VMEM_BYTES = 24 * 1024 * 1024


def shift_along(block, axis, distance):
    devices = range(lax.axis_size(axis))
    route = [(i - distance, i) for i in devices if i - distance in devices]
    return lax.ppermute(block, axis, route)


def whole(shape):
    return pl.BlockSpec(shape, lambda *_: (0,) * len(shape))


def column(row):
    return jnp.broadcast_to(row, (8, row.shape[1])).T[:, :1]


def rotated_rows(panels_ref, phases_ref, slots):
    rows_here, width = panels_ref.shape
    bins = width // 2
    pings = phases_ref.shape[1]
    count = slots.shape[1]
    slot_row = column(slots.astype(jnp.float32)).astype(jnp.int32)
    row_ids = lax.broadcasted_iota(jnp.int32, (count, rows_here), 1)
    pick = jnp.where(row_ids == slot_row, 1.0, 0.0).astype(jnp.bfloat16)
    picked = jnp.dot(pick, panels_ref[...], preferred_element_type=jnp.float32)
    phases = phases_ref[...]
    ping_ids = lax.broadcasted_iota(jnp.int32, (count, pings), 1)
    owned = ping_ids == (slot_row // (rows_here // pings))
    cos_col = jnp.sum(jnp.where(owned, jnp.cos(phases), 0.0), axis=1, keepdims=True)
    sin_col = jnp.sum(jnp.where(owned, jnp.sin(phases), 0.0), axis=1, keepdims=True)
    real_part = picked[:, :bins]
    imag_part = picked[:, bins:]
    return (
        (cos_col * real_part - sin_col * imag_part).astype(jnp.bfloat16),
        (sin_col * real_part + cos_col * imag_part).astype(jnp.bfloat16),
    )


def gather_rotated(panels, phases, slots, offsets):
    count = slots.shape[0] // 3
    width = panels.shape[1]
    bins = width // 2

    def kernel(panels_ref, phases_ref, slots_ref, *outs):
        for offset, out in zip(offsets, outs):
            real_part, imag_part = rotated_rows(
                panels_ref, phases_ref, slots_ref[:, pl.ds(offset * count, count)]
            )
            out[:, :bins] = real_part
            out[:, bins:] = imag_part

    return pl.pallas_call(
        kernel,
        out_shape=[jax.ShapeDtypeStruct((count, width), jnp.bfloat16) for _ in offsets],
        compiler_params=pltpu.CompilerParams(vmem_limit_bytes=VMEM_BYTES),
        name="gather_rotated",
    )(panels, phases.reshape(1, -1), slots.reshape(1, -1))


def make_table_kernel(ping_total, tile_total, track_groups, pixels, tile_devs, slots):
    def table_kernel(base_ref, counts_ref, slot_ref, ping_ref, base_cos, base_sin, step_cos, step_sin):
        tile = pl.program_id(0)
        foot = slot_ref.shape[2]
        count = counts_ref[tile]
        tile_global = base_ref[0] + tile
        slot_ids = lax.broadcasted_iota(jnp.int32, (slots, foot), 0)
        listed = slot_ref[0]
        group = slots // 3
        cap = group // tile_devs
        source = (listed % group) // cap
        placed = (source * 3 + listed // group) * cap + listed % cap
        match = jnp.where(slot_ids == placed, 1.0, 0.0).astype(jnp.bfloat16)
        pings = ping_ref[0]
        used = jnp.where(lax.broadcasted_iota(jnp.int32, (1, foot), 1) < count, 1.0, 0.0)
        values = jnp.concatenate(
            [
                (pings // HALF).astype(jnp.float32) * used,
                (pings % HALF).astype(jnp.float32) * used,
                used,
                jnp.zeros((5, foot), jnp.float32),
            ],
            axis=0,
        ).astype(jnp.bfloat16)
        found = lax.dot_general(
            match, values, (((1,), (1,)), ((), ())), preferred_element_type=jnp.float32
        )
        ping = (found[:, 0:1] * HALF + found[:, 1:2]).astype(jnp.int32)
        mask = found[:, 2:3]
        offset = (2 * ping + 1) * tile_total - (2 * tile_global + 1) * ping_total
        along = offset.astype(jnp.float32) * (track_groups / (2.0 * ping_total * tile_total))
        lane = lax.broadcasted_iota(jnp.int32, (1, LANES), 1).astype(jnp.float32)
        across = (lane + 0.5) / pixels - 0.5
        angle = 96.0 * across * along + 8.0 * (along * along)
        base_cos[0] = jnp.cos(angle) * mask
        base_sin[0] = jnp.sin(angle) * mask
        step = jnp.broadcast_to((96.0 * LANES / pixels) * along, (slots, 8))
        step_cos[0] = jnp.broadcast_to(jnp.cos(step)[:, :1], (slots, LANES))
        step_sin[0] = jnp.broadcast_to(jnp.sin(step)[:, :1], (slots, LANES))

    return table_kernel


def phase_tables(
    base, counts, foot_slot, foot_ping, slots, ping_total, tile_total, track_groups, tile_devs, pixels
):
    tiles_here, foot = foot_slot.shape
    kernel = make_table_kernel(ping_total, tile_total, track_groups, pixels, tile_devs, slots)
    table = jax.ShapeDtypeStruct((tiles_here, slots, LANES), jnp.float32)
    return pl.pallas_call(
        kernel,
        grid_spec=pltpu.PrefetchScalarGridSpec(
            num_scalar_prefetch=2,
            grid=(tiles_here,),
            in_specs=[pl.BlockSpec((1, 1, foot), lambda t, *_: (t, 0, 0))] * 2,
            out_specs=[pl.BlockSpec((1, slots, LANES), lambda t, *_: (t, 0, 0))] * 4,
        ),
        out_shape=[table] * 4,
        compiler_params=pltpu.CompilerParams(vmem_limit_bytes=VMEM_BYTES),
        name="phase_tables",
    )(base, counts, foot_slot.reshape(tiles_here, 1, foot), foot_ping.reshape(tiles_here, 1, foot))


def make_focus_kernel(slots, pixels, bins, tiles, chunk, piece):
    blocks = pixels // LANES
    chunks = slots // chunk

    def focus_kernel(
        class_ref, rows_ref, weight_hbm, base_c, base_s, step_c, step_s,
        image_ref, corr_ref, *scratch,
    ):
        turned_r, turned_i, corr_acc, weight_ref = scratch[2 * chunks : 2 * chunks + 4]
        tables_hbm = (base_c, base_s, step_c, step_s)
        tables = scratch[2 * chunks + 4 : 2 * chunks + 8]
        base_cos, base_sin, step_cos, step_sin = tables
        weight_sem, table_sem = scratch[2 * chunks + 8 :]

        def weight_copy(tile):
            return pltpu.make_async_copy(
                weight_hbm.at[class_ref[tile]], weight_ref.at[tile], weight_sem.at[tile]
            )

        def table_copies(tile):
            return [
                pltpu.make_async_copy(source.at[tile], target.at[tile], table_sem.at[tile, i])
                for i, (source, target) in enumerate(zip(tables_hbm, tables))
            ]

        for tile in range(tiles):
            weight_copy(tile).start()
            for copy in table_copies(tile):
                copy.start()

        def project(tile, part):
            for first in range(0, pixels, piece):
                for half in range(2):
                    scratch[2 * part + half][:, pl.ds(first, piece)] = lax.dot_general(
                        rows_ref[pl.ds(part * chunk, chunk), pl.ds(half * bins, bins)],
                        weight_ref[tile, pl.ds(first, piece), :],
                        (((1,), (1,)), ((), ())),
                        preferred_element_type=jnp.float32,
                    )

        def turn(tile, part, sums):
            sums = list(sums)
            for group in range(chunk // 8):
                local = pl.ds(group * 8, 8)
                at = pl.ds(part * chunk + group * 8, 8)
                cos_now = base_cos[tile, at, :]
                sin_now = base_sin[tile, at, :]
                turn_c = step_cos[tile, at, :]
                turn_s = step_sin[tile, at, :]
                for b in range(blocks):
                    lanes = pl.ds(b * LANES, LANES)
                    real = scratch[2 * part][local, lanes]
                    imag = scratch[2 * part + 1][local, lanes]
                    new_r = cos_now * real - sin_now * imag
                    new_i = sin_now * real + cos_now * imag
                    turned_r[at, lanes] = new_r
                    turned_i[at, lanes] = new_i
                    sums[2 * b] = sums[2 * b] + new_r
                    sums[2 * b + 1] = sums[2 * b + 1] + new_i
                    if b + 1 < blocks:
                        cos_now, sin_now = (
                            cos_now * turn_c - sin_now * turn_s,
                            sin_now * turn_c + cos_now * turn_s,
                        )
            return sums

        def one_tile(tile, _):
            sums = [jnp.zeros((8, LANES), jnp.float32)] * (2 * blocks)
            for copy in table_copies(tile):
                copy.wait()
            for part in range(chunks):
                following = tile
                if part + 1 == chunks:
                    following = jnp.minimum(tile + 1, tiles - 1)

                    @pl.when(tile + 1 < tiles)
                    def _():
                        weight_copy(tile + 1).wait()

                project(following, (part + 1) % chunks)
                sums = turn(tile, part, sums)
            heavy = []
            for b in range(blocks):
                lanes = pl.ds(b * LANES, LANES)
                real = jnp.sum(sums[2 * b], axis=0, keepdims=True)
                imag = jnp.sum(sums[2 * b + 1], axis=0, keepdims=True)
                image_ref[tile, 0:1, lanes] = real
                image_ref[tile, 1:2, lanes] = imag
                intensity = real * real + imag * imag
                heavy.append(jnp.broadcast_to(intensity * real, (8, LANES)))
                heavy.append(jnp.broadcast_to(intensity * imag, (8, LANES)))

            def pull(i, _):
                at = pl.ds(pl.multiple_of(i * 8, 8), 8)
                total = corr_acc[at, :]
                for b in range(blocks):
                    lanes = pl.ds(b * LANES, LANES)
                    total = total + (
                        turned_r[at, lanes] * heavy[2 * b + 1] - turned_i[at, lanes] * heavy[2 * b]
                    )
                corr_acc[at, :] = total
                return 0

            lax.fori_loop(0, slots // 8, pull, 0, unroll=4)
            return 0

        corr_acc[...] = jnp.zeros_like(corr_acc)
        weight_copy(0).wait()
        project(0, 0)
        lax.fori_loop(0, tiles, one_tile, 0)
        for part in range(slots // LANES):
            block = corr_acc[pl.ds(part * LANES, LANES), :]
            corr_ref[pl.ds(part, 1), :] = jnp.sum(block.T, axis=0, keepdims=True)

    return focus_kernel


def focus(tile_class, received, weight_tiles, tables, chunk, piece):
    slots, _ = received.shape
    _, pixels, bins = weight_tiles.shape
    tiles = tile_class.shape[0]
    parts = slots // LANES
    vmem = pl.BlockSpec(memory_space=pltpu.VMEM)
    image, corr = pl.pallas_call(
        make_focus_kernel(slots, pixels, bins, tiles, chunk, piece),
        in_specs=[pl.BlockSpec(memory_space=pltpu.SMEM), vmem]
        + [pl.BlockSpec(memory_space=pltpu.HBM)] * 5,
        out_specs=[vmem] * 2,
        scratch_shapes=[pltpu.VMEM((chunk, pixels), jnp.float32)] * (2 * (slots // chunk))
        + [
            pltpu.VMEM((slots, pixels), jnp.float32),
            pltpu.VMEM((slots, pixels), jnp.float32),
            pltpu.VMEM((slots, LANES), jnp.float32),
            pltpu.VMEM((tiles, pixels, bins), jnp.bfloat16),
        ]
        + [pltpu.VMEM((tiles, slots, LANES), jnp.float32)] * 4
        + [pltpu.SemaphoreType.DMA((tiles,)), pltpu.SemaphoreType.DMA((tiles, 4))],
        out_shape=[
            jax.ShapeDtypeStruct((tiles, 2, pixels), jnp.float32),
            jax.ShapeDtypeStruct((parts, LANES), jnp.float32),
        ],
        compiler_params=pltpu.CompilerParams(vmem_limit_bytes=48 * 1024 * 1024),
        name="focus",
    )(tile_class, received, weight_tiles, *tables)
    return image, corr.reshape(slots)


def on_device(
    panels, phases, weight_tiles, tile_class, send_slots, foot_slot, foot_ping, tile_counts
):
    track_devs = lax.axis_size("track")
    tile_devs = lax.axis_size("tile")
    device = lax.axis_index("track") * tile_devs + lax.axis_index("tile")
    ping_local = phases.shape[0]
    row_width = panels.shape[1]
    tiles_here = tile_counts.shape[0]
    pixels = weight_tiles.shape[1]
    slots = send_slots.shape[0]
    slot_cap = slots // 3 // tile_devs
    ping_total = ping_local * track_devs * tile_devs
    tile_total = tiles_here * track_devs * tile_devs

    blocks = (tile_devs, slot_cap, row_width)
    to_next, to_last = gather_rotated(panels, phases, send_slots, (2, 0))
    behind = shift_along(to_next.reshape(blocks), "track", 1)
    ahead = shift_along(to_last.reshape(blocks), "track", -1)
    (own,) = gather_rotated(panels, phases, send_slots, (1,))
    mixed = jnp.concatenate([behind, own.reshape(blocks), ahead], axis=1)
    arrived = lax.all_to_all(mixed, "tile", split_axis=0, concat_axis=0, tiled=True)
    tables = phase_tables(
        (device * tiles_here).astype(jnp.int32).reshape(1),
        tile_counts, foot_slot, foot_ping, slots,
        ping_total, tile_total, track_devs, tile_devs, pixels,
    )
    image, corr = focus(
        tile_class, arrived.reshape(slots, row_width), weight_tiles, tables, slots // 3, 256
    )

    partial = corr.reshape(tile_devs, 3, slot_cap)
    behind = shift_along(partial[:, 2], "track", 1)
    ahead = shift_along(partial[:, 0], "track", -1)
    back = jnp.concatenate([behind, partial[:, 1], ahead], axis=1)
    back = lax.all_to_all(back, "tile", split_axis=0, concat_axis=0, tiled=True)
    back = back.reshape(tile_devs, 3, slot_cap).transpose(1, 0, 2).reshape(1, slots)
    owner = (send_slots // (panels.shape[0] // ping_local)).reshape(1, slots)
    mine = lax.broadcasted_iota(jnp.int32, (ping_local, slots), 0) == owner
    ping_gradient = jnp.sum(jnp.where(mine & (send_slots >= 0)[None, :], back, 0.0), axis=1)
    return (image, ping_gradient)


def solution(mesh):
    spread = P(("track", "tile"))
    in_specs = (
        P(("track", "tile"), None), spread, P(), spread, spread,
        P(("track", "tile"), None), P(("track", "tile"), None), spread,
    )
    out_specs = (P(("track", "tile"), None, None), spread)
    return jax.shard_map(
        on_device, mesh=mesh, in_specs=in_specs, out_specs=out_specs, check_vma=False
    )
```

```python
import functools
import math

import jax
import jax.numpy as jnp
from jax import lax
from jax.experimental import pallas as pl
from jax.experimental.pallas import tpu as pltpu
from jax.sharding import PartitionSpec as P

LANES = 128
HALF = 128
VMEM_BYTES = 24 * 1024 * 1024
ALL_VMEM = 60 * 1024 * 1024


def shift_along(block, axis, distance):
    devices = range(lax.axis_size(axis))
    route = [(i - distance, i) for i in devices if i - distance in devices]
    return lax.ppermute(block, axis, route)


def whole(shape):
    return pl.BlockSpec(shape, lambda *_: (0,) * len(shape))


def column(row):
    return jnp.broadcast_to(row, (8, row.shape[1])).T[:, :1]


def rotated_rows(panels_ref, phases_ref, slots):
    rows_here, width = panels_ref.shape
    bins = width // 2
    pings = phases_ref.shape[1]
    count = slots.shape[1]
    slot_row = column(slots.astype(jnp.float32)).astype(jnp.int32)
    row_ids = lax.broadcasted_iota(jnp.int32, (count, rows_here), 1)
    pick = jnp.where(row_ids == slot_row, 1.0, 0.0).astype(jnp.bfloat16)
    picked = jnp.dot(pick, panels_ref[...], preferred_element_type=jnp.float32)
    phases = phases_ref[...]
    ping_ids = lax.broadcasted_iota(jnp.int32, (count, pings), 1)
    owned = ping_ids == (slot_row // (rows_here // pings))
    cos_col = jnp.sum(jnp.where(owned, jnp.cos(phases), 0.0), axis=1, keepdims=True)
    sin_col = jnp.sum(jnp.where(owned, jnp.sin(phases), 0.0), axis=1, keepdims=True)
    real_part = picked[:, :bins]
    imag_part = picked[:, bins:]
    return (
        (cos_col * real_part - sin_col * imag_part).astype(jnp.bfloat16),
        (sin_col * real_part + cos_col * imag_part).astype(jnp.bfloat16),
    )


def gather_rotated(panels, phases, slots, offsets):
    count = slots.shape[0] // 3
    width = panels.shape[1]
    bins = width // 2

    def kernel(panels_ref, phases_ref, slots_ref, *outs):
        for offset, out in zip(offsets, outs):
            real_part, imag_part = rotated_rows(
                panels_ref, phases_ref, slots_ref[:, pl.ds(offset * count, count)]
            )
            out[:, :bins] = real_part
            out[:, bins:] = imag_part

    return pl.pallas_call(
        kernel,
        out_shape=[jax.ShapeDtypeStruct((count, width), jnp.bfloat16) for _ in offsets],
        compiler_params=pltpu.CompilerParams(vmem_limit_bytes=VMEM_BYTES),
        name="gather_rotated",
    )(panels, phases.reshape(1, -1), slots.reshape(1, -1))


def cos_sin(angle):
    turns = jnp.round(angle * (2.0 / math.pi))
    rest = angle - turns * 1.5703125
    rest = rest - turns * 4.837512969970703125e-4
    rest = rest - turns * 7.549789948768648e-8
    square = rest * rest
    sine = (-1.9515295891e-4 * square + 8.3321608736e-3) * square - 1.6666654611e-1
    sine = sine * square * rest + rest
    cosine = (2.443315711809948e-5 * square - 1.388731625493765e-3) * square
    cosine = (cosine + 4.166664568298827e-2) * square * square - 0.5 * square + 1.0
    quarter = turns.astype(jnp.int32)
    odd = (quarter & 1) == 1
    cos_out = jnp.where(odd, sine, cosine)
    sin_out = jnp.where(odd, cosine, sine)
    cos_out = jnp.where(((quarter + 1) & 2) == 2, -cos_out, cos_out)
    sin_out = jnp.where((quarter & 2) == 2, -sin_out, sin_out)
    return cos_out, sin_out


def make_table_kernel(ping_total, tile_total, track_groups, pixels, tile_devs, slots, tiles):
    def table_kernel(base_ref, counts_ref, slot_ref, ping_ref, base_cos, base_sin, step_cos, step_sin):
        foot = slot_ref.shape[1]
        group = slots // 3
        cap = group // tile_devs
        slot_ids = lax.broadcasted_iota(jnp.int32, (slots, foot), 0)
        lane = lax.broadcasted_iota(jnp.int32, (1, LANES), 1)
        across = (lane.astype(jnp.float32) + 0.5) / pixels - 0.5
        step_angle = jnp.zeros((slots, LANES), jnp.float32)
        for tile in range(tiles):
            listed = slot_ref[tile : tile + 1, :]
            offset = listed // group
            source = (listed % group) // cap
            place = listed % cap
            placed = jnp.where(
                offset == 1,
                2 * group + source * cap + place,
                (source * 2 + offset // 2) * cap + place,
            )
            match = jnp.where(slot_ids == placed, 1.0, 0.0).astype(jnp.bfloat16)
            pings = ping_ref[tile : tile + 1, :]
            entry = lax.broadcasted_iota(jnp.int32, (1, foot), 1)
            used = jnp.where(entry < counts_ref[tile], 1.0, 0.0)
            values = jnp.concatenate(
                [
                    (pings // HALF).astype(jnp.float32) * used,
                    (pings % HALF).astype(jnp.float32) * used,
                    used,
                    jnp.zeros((5, foot), jnp.float32),
                ],
                axis=0,
            ).astype(jnp.bfloat16)
            found = lax.dot_general(
                match, values, (((1,), (1,)), ((), ())), preferred_element_type=jnp.float32
            )
            ping = (found[:, 0:1] * HALF + found[:, 1:2]).astype(jnp.int32)
            mask = found[:, 2:3]
            gap = (2 * ping + 1) * tile_total - (2 * (base_ref[0] + tile) + 1) * ping_total
            along = gap.astype(jnp.float32) * (track_groups / (2.0 * ping_total * tile_total))
            cosine, sine = cos_sin(96.0 * across * along + 8.0 * (along * along))
            base_cos[tile] = cosine * mask
            base_sin[tile] = sine * mask
            step_angle = jnp.where(lane == tile, (96.0 * LANES / pixels) * along, step_angle)
        cosine, sine = cos_sin(step_angle)
        for tile in range(tiles):
            step_cos[tile] = jnp.broadcast_to(cosine[:, tile : tile + 1], (slots, LANES))
            step_sin[tile] = jnp.broadcast_to(sine[:, tile : tile + 1], (slots, LANES))

    return table_kernel


def phase_tables(
    base, counts, foot_slot, foot_ping, slots, ping_total, tile_total, track_groups, tile_devs, pixels
):
    tiles, foot = foot_slot.shape
    kernel = make_table_kernel(ping_total, tile_total, track_groups, pixels, tile_devs, slots, tiles)
    table = jax.ShapeDtypeStruct((tiles, slots, LANES), jnp.float32)
    smem = pl.BlockSpec(memory_space=pltpu.SMEM)
    vmem = pl.BlockSpec(memory_space=pltpu.VMEM)
    return pl.pallas_call(
        kernel,
        in_specs=[smem, smem, vmem, vmem],
        out_specs=[vmem] * 4,
        out_shape=[table] * 4,
        compiler_params=pltpu.CompilerParams(vmem_limit_bytes=ALL_VMEM),
        name="phase_tables",
    )(base, counts, foot_slot, foot_ping)


def turn_rows(real_ref, imag_ref, rows, cos_now, sin_now, turn_c, turn_s, out_r, out_i, sums):
    blocks = len(sums) // 2
    sums = list(sums)
    for b in range(blocks):
        lanes = pl.ds(b * LANES, LANES)
        real = real_ref[rows, lanes]
        imag = imag_ref[rows, lanes]
        new_r = cos_now * real - sin_now * imag
        new_i = sin_now * real + cos_now * imag
        out_r(lanes, new_r)
        out_i(lanes, new_i)
        sums[2 * b] = sums[2 * b] + new_r
        sums[2 * b + 1] = sums[2 * b + 1] + new_i
        if b + 1 < blocks:
            cos_now, sin_now = (
                cos_now * turn_c - sin_now * turn_s,
                sin_now * turn_c + cos_now * turn_s,
            )
    return sums


def project_rows(rows_ref, first_row, count, weight, out_r, out_i, bins, pixels, piece):
    for first in range(0, pixels, piece):
        for half, out in enumerate((out_r, out_i)):
            out[:, pl.ds(first, piece)] = lax.dot_general(
                rows_ref[pl.ds(first_row, count), pl.ds(half * bins, bins)],
                weight(first, piece),
                (((1,), (1,)), ((), ())),
                preferred_element_type=jnp.float32,
            )


def own_forward(tile_class, own, weight_tiles, tables, first_slot):
    count, width = own.shape
    _, pixels, bins = weight_tiles.shape
    tiles = tile_class.shape[0]
    blocks = pixels // LANES
    block_at = first_slot // count

    def kernel(class_ref, rows_ref, weight_ref, base_c, base_s, step_c, step_s, turned_r, turned_i, sums_ref, proj_r, proj_i):
        project_rows(
            rows_ref, 0, count, lambda first, size: weight_ref[0, pl.ds(first, size), :],
            proj_r, proj_i, bins, pixels, pixels,
        )

        def group(i, sums):
            at = pl.ds(pl.multiple_of(i * 8, 8), 8)

            def put(ref):
                def store(lanes, value):
                    ref[0, at, lanes] = value

                return store

            return tuple(
                turn_rows(
                    proj_r, proj_i, at, base_c[0, at, :], base_s[0, at, :], step_c[0, at, :],
                    step_s[0, at, :], put(turned_r), put(turned_i), sums,
                )
            )

        sums = (jnp.zeros((8, LANES), jnp.float32),) * (2 * blocks)
        sums = lax.fori_loop(0, count // 8, group, sums, unroll=4)
        for b in range(blocks):
            for half in range(2):
                sums_ref[0, half, :, pl.ds(b * LANES, LANES)] = sums[2 * b + half]

    table_spec = pl.BlockSpec((1, count, LANES), lambda t, *_: (t, block_at, 0))
    turned = jax.ShapeDtypeStruct((tiles, count, pixels), jnp.float32)
    turned_spec = pl.BlockSpec((1, count, pixels), lambda t, *_: (t, 0, 0))
    return pl.pallas_call(
        kernel,
        grid_spec=pltpu.PrefetchScalarGridSpec(
            num_scalar_prefetch=1,
            grid=(tiles,),
            in_specs=[
                pl.BlockSpec((count, width), lambda t, *_: (0, 0)),
                pl.BlockSpec((1, pixels, bins), lambda t, cls: (cls[t], 0, 0)),
            ]
            + [table_spec] * 4,
            out_specs=[
                turned_spec,
                turned_spec,
                pl.BlockSpec((1, 2, 8, pixels), lambda t, *_: (t, 0, 0, 0)),
            ],
            scratch_shapes=[pltpu.VMEM((count, pixels), jnp.float32)] * 2,
        ),
        out_shape=[turned, turned, jax.ShapeDtypeStruct((tiles, 2, 8, pixels), jnp.float32)],
        compiler_params=pltpu.CompilerParams(vmem_limit_bytes=ALL_VMEM),
        name="own_forward",
    )(tile_class, own, weight_tiles, *tables)


def make_focus_kernel(mixed, own, pixels, bins, tiles, chunk, piece):
    blocks = pixels // LANES
    chunks = mixed // chunk

    def focus_kernel(
        class_ref, rows_ref, sums_ref, weight_hbm, base_c, base_s, step_c, step_s, own_r, own_i,
        image_ref, corr_ref, *scratch,
    ):
        proj = scratch[: 2 * chunks]
        turned_r, turned_i, corr_acc, weight_ref = scratch[2 * chunks : 2 * chunks + 4]
        base_cos, base_sin, step_cos, step_sin, far_r, far_i = scratch[
            2 * chunks + 4 : 2 * chunks + 10
        ]
        weight_sem, table_sem, own_sem = scratch[2 * chunks + 10 :]

        def weight_copy(tile):
            return pltpu.make_async_copy(
                weight_hbm.at[class_ref[tile]], weight_ref.at[tile], weight_sem.at[tile]
            )

        def table_copies(tile):
            pairs = (base_c, base_cos), (base_s, base_sin), (step_c, step_cos), (step_s, step_sin)
            return [
                pltpu.make_async_copy(
                    source.at[tile, pl.ds(0, mixed)], target.at[tile], table_sem.at[tile, i]
                )
                for i, (source, target) in enumerate(pairs)
            ]

        def own_copies(tile):
            return [
                pltpu.make_async_copy(source.at[tile], target.at[tile], own_sem.at[tile, i])
                for i, (source, target) in enumerate(((own_r, far_r), (own_i, far_i)))
            ]

        for tile in range(tiles):
            for copy in [weight_copy(tile)] + table_copies(tile) + own_copies(tile):
                copy.start()

        def project(tile, part):
            project_rows(
                rows_ref, part * chunk, chunk,
                lambda first, size: weight_ref[tile, pl.ds(first, size), :],
                proj[2 * part], proj[2 * part + 1], bins, pixels, piece,
            )

        def turn(tile, part, sums):
            for group in range(chunk // 8):
                at = pl.ds(part * chunk + group * 8, 8)

                def put(ref, at=at):
                    def store(lanes, value):
                        ref[at, lanes] = value

                    return store

                sums = turn_rows(
                    proj[2 * part], proj[2 * part + 1], pl.ds(group * 8, 8),
                    base_cos[tile, at, :], base_sin[tile, at, :],
                    step_cos[tile, at, :], step_sin[tile, at, :],
                    put(turned_r), put(turned_i), sums,
                )
            return sums

        def one_tile(tile, _):
            sums = []
            for b in range(blocks):
                for half in range(2):
                    sums.append(sums_ref[tile, half, :, pl.ds(b * LANES, LANES)])
            for copy in table_copies(tile):
                copy.wait()
            for part in range(chunks):
                following = tile
                if part + 1 == chunks:
                    following = jnp.minimum(tile + 1, tiles - 1)

                    @pl.when(tile + 1 < tiles)
                    def _():
                        weight_copy(tile + 1).wait()

                project(following, (part + 1) % chunks)
                sums = turn(tile, part, sums)
            heavy = []
            for b in range(blocks):
                lanes = pl.ds(b * LANES, LANES)
                real = jnp.sum(sums[2 * b], axis=0, keepdims=True)
                imag = jnp.sum(sums[2 * b + 1], axis=0, keepdims=True)
                image_ref[tile, 0:1, lanes] = real
                image_ref[tile, 1:2, lanes] = imag
                intensity = real * real + imag * imag
                heavy.append(jnp.broadcast_to(intensity * real, (8, LANES)))
                heavy.append(jnp.broadcast_to(intensity * imag, (8, LANES)))
            for copy in own_copies(tile):
                copy.wait()

            def pull(i, _, real_of, imag_of, first):
                row = pl.multiple_of(i * 8, 8)
                at = pl.ds(pl.multiple_of(first + i * 8, 8), 8)
                total = corr_acc[at, :]
                for b in range(blocks):
                    lanes = pl.ds(b * LANES, LANES)
                    total = total + (
                        real_of(row, lanes) * heavy[2 * b + 1] - imag_of(row, lanes) * heavy[2 * b]
                    )
                corr_acc[at, :] = total
                return 0

            near = functools.partial(
                pull,
                real_of=lambda row, lanes: turned_r[pl.ds(row, 8), lanes],
                imag_of=lambda row, lanes: turned_i[pl.ds(row, 8), lanes],
                first=0,
            )
            far = functools.partial(
                pull,
                real_of=lambda row, lanes: far_r[tile, pl.ds(row, 8), lanes],
                imag_of=lambda row, lanes: far_i[tile, pl.ds(row, 8), lanes],
                first=mixed,
            )
            lax.fori_loop(0, mixed // 8, near, 0, unroll=4)
            lax.fori_loop(0, own // 8, far, 0, unroll=4)
            return 0

        corr_acc[...] = jnp.zeros_like(corr_acc)
        weight_copy(0).wait()
        project(0, 0)
        lax.fori_loop(0, tiles, one_tile, 0)
        for part in range((mixed + own) // LANES):
            block = corr_acc[pl.ds(part * LANES, LANES), :]
            corr_ref[pl.ds(part, 1), :] = jnp.sum(block.T, axis=0, keepdims=True)

    return focus_kernel


def focus(tile_class, arrived, weight_tiles, tables, own_parts, chunk, piece):
    turned_own_r, turned_own_i, own_sums = own_parts
    mixed, _ = arrived.shape
    own = turned_own_r.shape[1]
    slots = mixed + own
    _, pixels, bins = weight_tiles.shape
    tiles = tile_class.shape[0]
    vmem = pl.BlockSpec(memory_space=pltpu.VMEM)
    hbm = pl.BlockSpec(memory_space=pltpu.HBM)
    image, corr = pl.pallas_call(
        make_focus_kernel(mixed, own, pixels, bins, tiles, chunk, piece),
        in_specs=[pl.BlockSpec(memory_space=pltpu.SMEM), vmem, vmem] + [hbm] * 7,
        out_specs=[vmem] * 2,
        scratch_shapes=[pltpu.VMEM((chunk, pixels), jnp.float32)] * (2 * (mixed // chunk))
        + [
            pltpu.VMEM((mixed, pixels), jnp.float32),
            pltpu.VMEM((mixed, pixels), jnp.float32),
            pltpu.VMEM((slots, LANES), jnp.float32),
            pltpu.VMEM((tiles, pixels, bins), jnp.bfloat16),
        ]
        + [pltpu.VMEM((tiles, mixed, LANES), jnp.float32)] * 4
        + [pltpu.VMEM((tiles, own, pixels), jnp.float32)] * 2
        + [
            pltpu.SemaphoreType.DMA((tiles,)),
            pltpu.SemaphoreType.DMA((tiles, 4)),
            pltpu.SemaphoreType.DMA((tiles, 2)),
        ],
        out_shape=[
            jax.ShapeDtypeStruct((tiles, 2, pixels), jnp.float32),
            jax.ShapeDtypeStruct((slots // LANES, LANES), jnp.float32),
        ],
        compiler_params=pltpu.CompilerParams(vmem_limit_bytes=ALL_VMEM),
        name="focus",
    )(tile_class, arrived, own_sums, weight_tiles, *tables, turned_own_r, turned_own_i)
    return image, corr.reshape(slots)


def on_device(
    panels, phases, weight_tiles, tile_class, send_slots, foot_slot, foot_ping, tile_counts
):
    track_devs = lax.axis_size("track")
    tile_devs = lax.axis_size("tile")
    device = lax.axis_index("track") * tile_devs + lax.axis_index("tile")
    ping_local = phases.shape[0]
    row_width = panels.shape[1]
    tiles_here = tile_counts.shape[0]
    pixels = weight_tiles.shape[1]
    slots = send_slots.shape[0]
    slot_cap = slots // 3 // tile_devs
    ping_total = ping_local * track_devs * tile_devs
    tile_total = tiles_here * track_devs * tile_devs

    blocks = (tile_devs, slot_cap, row_width)
    group = slots // 3
    (own,) = gather_rotated(panels, phases, send_slots, (1,))
    own_arrived = lax.all_to_all(
        own.reshape(blocks), "tile", split_axis=0, concat_axis=0, tiled=True
    )
    to_next, to_last = gather_rotated(panels, phases, send_slots, (2, 0))
    behind = shift_along(to_next.reshape(blocks), "track", 1)
    ahead = shift_along(to_last.reshape(blocks), "track", -1)
    mixed = jnp.concatenate([behind, ahead], axis=1)
    mixed, own_arrived = lax.optimization_barrier((mixed, own_arrived))
    arrived = lax.all_to_all(mixed, "tile", split_axis=0, concat_axis=0, tiled=True)
    tables = phase_tables(
        (device * tiles_here).astype(jnp.int32).reshape(1),
        tile_counts, foot_slot, foot_ping, slots,
        ping_total, tile_total, track_devs, tile_devs, pixels,
    )
    own_parts = own_forward(
        tile_class, own_arrived.reshape(group, row_width), weight_tiles, tables, 2 * group
    )
    image, corr = focus(
        tile_class, arrived.reshape(2 * group, row_width), weight_tiles, tables, own_parts, group, 256
    )

    partial = corr[: 2 * group].reshape(tile_devs, 2, slot_cap)
    near = corr[2 * group :].reshape(tile_devs, slot_cap)
    behind = shift_along(partial[:, 1], "track", 1)
    ahead = shift_along(partial[:, 0], "track", -1)
    back = jnp.concatenate([behind, near, ahead], axis=1)
    back = lax.all_to_all(back, "tile", split_axis=0, concat_axis=0, tiled=True)
    back = back.reshape(tile_devs, 3, slot_cap).transpose(1, 0, 2).reshape(1, slots)
    owner = (send_slots // (panels.shape[0] // ping_local)).reshape(1, slots)
    mine = lax.broadcasted_iota(jnp.int32, (ping_local, slots), 0) == owner
    ping_gradient = jnp.sum(jnp.where(mine & (send_slots >= 0)[None, :], back, 0.0), axis=1)
    return (image, ping_gradient)


def solution(mesh):
    spread = P(("track", "tile"))
    in_specs = (
        P(("track", "tile"), None), spread, P(), spread, spread,
        P(("track", "tile"), None), P(("track", "tile"), None), spread,
    )
    out_specs = (P(("track", "tile"), None, None), spread)
    return jax.shard_map(
        on_device, mesh=mesh, in_specs=in_specs, out_specs=out_specs, check_vma=False
    )
```

```python
import functools
import math

import jax
import jax.numpy as jnp
from jax import lax
from jax.experimental import pallas as pl
from jax.experimental.pallas import tpu as pltpu
from jax.sharding import PartitionSpec as P

LANES = 128
HALF = 128
ALL_VMEM = 60 * 1024 * 1024


def shift_along(block, axis, distance):
    devices = range(lax.axis_size(axis))
    route = [(i - distance, i) for i in devices if i - distance in devices]
    return lax.ppermute(block, axis, route)


def whole(shape):
    return pl.BlockSpec(shape, lambda *_: (0,) * len(shape))


def column(row):
    return jnp.broadcast_to(row, (8, row.shape[1])).T[:, :1]


def rotated_rows(panels_ref, phases_ref, slots_ref, first, count):
    rows_here, width = panels_ref.shape
    bins = width // 2
    pings = phases_ref.shape[1]
    columns = [
        column(slots_ref[pl.ds(row, 1), :].astype(jnp.float32))
        for row in range(first // LANES, (first + count) // LANES)
    ]
    slot_row = jnp.concatenate(columns, axis=0).astype(jnp.int32)
    row_ids = lax.broadcasted_iota(jnp.int32, (count, rows_here), 1)
    pick = jnp.where(row_ids == slot_row, 1.0, 0.0).astype(jnp.bfloat16)
    picked = jnp.dot(pick, panels_ref[...], preferred_element_type=jnp.float32)
    phases = phases_ref[...]
    ping_ids = lax.broadcasted_iota(jnp.int32, (count, pings), 1)
    owned = ping_ids == (slot_row // (rows_here // pings))
    cos_col = jnp.sum(jnp.where(owned, jnp.cos(phases), 0.0), axis=1, keepdims=True)
    sin_col = jnp.sum(jnp.where(owned, jnp.sin(phases), 0.0), axis=1, keepdims=True)
    real_part = picked[:, :bins]
    imag_part = picked[:, bins:]
    return (
        (cos_col * real_part - sin_col * imag_part).astype(jnp.bfloat16),
        (sin_col * real_part + cos_col * imag_part).astype(jnp.bfloat16),
    )


def gather_rotated(panels, phases, slots, offsets):
    count = slots.shape[0] // 3
    width = panels.shape[1]
    bins = width // 2

    def kernel(panels_ref, phases_ref, slots_ref, *outs):
        for offset, out in zip(offsets, outs):
            real_part, imag_part = rotated_rows(
                panels_ref, phases_ref, slots_ref, offset * count, count
            )
            out[:, :bins] = real_part
            out[:, bins:] = imag_part

    return pl.pallas_call(
        kernel,
        out_shape=[jax.ShapeDtypeStruct((count, width), jnp.bfloat16) for _ in offsets],
        compiler_params=pltpu.CompilerParams(vmem_limit_bytes=ALL_VMEM),
        name="gather_rotated",
    )(panels, phases.reshape(1, -1), slots.reshape(-1, LANES))


def cos_sin(angle):
    turns = jnp.round(angle * (2.0 / math.pi))
    rest = angle - turns * 1.5703125
    rest = rest - turns * 4.837512969970703125e-4
    rest = rest - turns * 7.549789948768648e-8
    square = rest * rest
    sine = (-1.9515295891e-4 * square + 8.3321608736e-3) * square - 1.6666654611e-1
    sine = sine * square * rest + rest
    cosine = (2.443315711809948e-5 * square - 1.388731625493765e-3) * square
    cosine = (cosine + 4.166664568298827e-2) * square * square - 0.5 * square + 1.0
    quarter = turns.astype(jnp.int32)
    odd = (quarter & 1) == 1
    cos_out = jnp.where(odd, sine, cosine)
    sin_out = jnp.where(odd, cosine, sine)
    cos_out = jnp.where(((quarter + 1) & 2) == 2, -cos_out, cos_out)
    sin_out = jnp.where((quarter & 2) == 2, -sin_out, sin_out)
    return cos_out, sin_out


def make_table_kernel(ping_total, tile_total, track_groups, pixels, tile_devs, slots, tiles):
    def table_kernel(base_ref, counts_ref, slot_ref, ping_ref, base_cos, base_sin, step_cos, step_sin):
        foot = slot_ref.shape[1]
        group = slots // 3
        cap = group // tile_devs
        slot_ids = lax.broadcasted_iota(jnp.int32, (slots, foot), 0)
        lane = lax.broadcasted_iota(jnp.int32, (1, LANES), 1)
        across = (lane.astype(jnp.float32) + 0.5) / pixels - 0.5
        step_angle = jnp.zeros((slots, LANES), jnp.float32)
        for tile in range(tiles):
            listed = slot_ref[tile : tile + 1, :]
            offset = listed // group
            source = (listed % group) // cap
            place = listed % cap
            placed = jnp.where(
                offset == 1,
                2 * group + source * cap + place,
                (source * 2 + offset // 2) * cap + place,
            )
            match = jnp.where(slot_ids == placed, 1.0, 0.0).astype(jnp.bfloat16)
            pings = ping_ref[tile : tile + 1, :]
            entry = lax.broadcasted_iota(jnp.int32, (1, foot), 1)
            used = jnp.where(entry < counts_ref[tile], 1.0, 0.0)
            values = jnp.concatenate(
                [
                    (pings // HALF).astype(jnp.float32) * used,
                    (pings % HALF).astype(jnp.float32) * used,
                    used,
                    jnp.zeros((5, foot), jnp.float32),
                ],
                axis=0,
            ).astype(jnp.bfloat16)
            found = lax.dot_general(
                match, values, (((1,), (1,)), ((), ())), preferred_element_type=jnp.float32
            )
            ping = (found[:, 0:1] * HALF + found[:, 1:2]).astype(jnp.int32)
            mask = found[:, 2:3]
            gap = (2 * ping + 1) * tile_total - (2 * (base_ref[0] + tile) + 1) * ping_total
            along = gap.astype(jnp.float32) * (track_groups / (2.0 * ping_total * tile_total))
            cosine, sine = cos_sin(96.0 * across * along + 8.0 * (along * along))
            base_cos[tile] = cosine * mask
            base_sin[tile] = sine * mask
            step_angle = jnp.where(lane == tile, (96.0 * LANES / pixels) * along, step_angle)
        cosine, sine = cos_sin(step_angle)
        for tile in range(tiles):
            step_cos[tile] = jnp.broadcast_to(cosine[:, tile : tile + 1], (slots, LANES))
            step_sin[tile] = jnp.broadcast_to(sine[:, tile : tile + 1], (slots, LANES))

    return table_kernel


def phase_tables(
    base, counts, foot_slot, foot_ping, slots, ping_total, tile_total, track_groups, tile_devs, pixels
):
    tiles, foot = foot_slot.shape
    kernel = make_table_kernel(ping_total, tile_total, track_groups, pixels, tile_devs, slots, tiles)
    table = jax.ShapeDtypeStruct((tiles, slots, LANES), jnp.float32)
    smem = pl.BlockSpec(memory_space=pltpu.SMEM)
    vmem = pl.BlockSpec(memory_space=pltpu.VMEM)
    return pl.pallas_call(
        kernel,
        in_specs=[smem, smem, vmem, vmem],
        out_specs=[vmem] * 4,
        out_shape=[table] * 4,
        compiler_params=pltpu.CompilerParams(vmem_limit_bytes=ALL_VMEM),
        name="phase_tables",
    )(base, counts, foot_slot, foot_ping)


def turn_rows(real_ref, imag_ref, rows, cos_now, sin_now, turn_c, turn_s, out_r, out_i, sums):
    blocks = len(sums) // 2
    sums = list(sums)
    for b in range(blocks):
        lanes = pl.ds(b * LANES, LANES)
        real = real_ref[rows, lanes]
        imag = imag_ref[rows, lanes]
        new_r = cos_now * real - sin_now * imag
        new_i = sin_now * real + cos_now * imag
        out_r(lanes, new_r)
        out_i(lanes, new_i)
        sums[2 * b] = sums[2 * b] + new_r
        sums[2 * b + 1] = sums[2 * b + 1] + new_i
        if b + 1 < blocks:
            cos_now, sin_now = (
                cos_now * turn_c - sin_now * turn_s,
                sin_now * turn_c + cos_now * turn_s,
            )
    return sums


def project_rows(rows_ref, first_row, count, weight, out_r, out_i, bins, pixels, piece):
    for first in range(0, pixels, piece):
        for half, out in enumerate((out_r, out_i)):
            out[:, pl.ds(first, piece)] = lax.dot_general(
                rows_ref[pl.ds(first_row, count), pl.ds(half * bins, bins)],
                weight(first, piece),
                (((1,), (1,)), ((), ())),
                preferred_element_type=jnp.float32,
            )


def own_forward(tile_class, own, weight_tiles, tables, first_slot):
    count, width = own.shape
    _, pixels, bins = weight_tiles.shape
    tiles = tile_class.shape[0]
    blocks = pixels // LANES
    block_at = first_slot // count

    def kernel(class_ref, rows_ref, weight_ref, base_c, base_s, step_c, step_s, turned_r, turned_i, sums_ref, proj_r, proj_i):
        project_rows(
            rows_ref, 0, count, lambda first, size: weight_ref[0, pl.ds(first, size), :],
            proj_r, proj_i, bins, pixels, pixels,
        )

        def group(i, sums):
            at = pl.ds(pl.multiple_of(i * 8, 8), 8)

            def put(ref):
                def store(lanes, value):
                    ref[0, at, lanes] = value

                return store

            return tuple(
                turn_rows(
                    proj_r, proj_i, at, base_c[0, at, :], base_s[0, at, :], step_c[0, at, :],
                    step_s[0, at, :], put(turned_r), put(turned_i), sums,
                )
            )

        sums = (jnp.zeros((8, LANES), jnp.float32),) * (2 * blocks)
        sums = lax.fori_loop(0, count // 8, group, sums, unroll=4)
        for b in range(blocks):
            for half in range(2):
                sums_ref[0, half, :, pl.ds(b * LANES, LANES)] = sums[2 * b + half]

    table_spec = pl.BlockSpec((1, count, LANES), lambda t, *_: (t, block_at, 0))
    turned = jax.ShapeDtypeStruct((tiles, count, pixels), jnp.float32)
    turned_spec = pl.BlockSpec((1, count, pixels), lambda t, *_: (t, 0, 0))
    return pl.pallas_call(
        kernel,
        grid_spec=pltpu.PrefetchScalarGridSpec(
            num_scalar_prefetch=1,
            grid=(tiles,),
            in_specs=[
                pl.BlockSpec((count, width), lambda t, *_: (0, 0)),
                pl.BlockSpec((1, pixels, bins), lambda t, cls: (cls[t], 0, 0)),
            ]
            + [table_spec] * 4,
            out_specs=[
                turned_spec,
                turned_spec,
                pl.BlockSpec((1, 2, 8, pixels), lambda t, *_: (t, 0, 0, 0)),
            ],
            scratch_shapes=[pltpu.VMEM((count, pixels), jnp.float32)] * 2,
        ),
        out_shape=[turned, turned, jax.ShapeDtypeStruct((tiles, 2, 8, pixels), jnp.float32)],
        compiler_params=pltpu.CompilerParams(vmem_limit_bytes=ALL_VMEM),
        name="own_forward",
    )(tile_class, own, weight_tiles, *tables)


def make_focus_kernel(mixed, own, pixels, bins, tiles, chunk, piece):
    blocks = pixels // LANES
    chunks = mixed // chunk

    def focus_kernel(
        class_ref, rows_ref, sums_ref, weight_ref, base_c, base_s, step_c, step_s, own_r, own_i,
        image_ref, corr_ref, *scratch,
    ):
        proj = scratch[: 2 * chunks]
        turned_r, turned_i, corr_acc = scratch[2 * chunks : 2 * chunks + 3]
        base_cos, base_sin, step_cos, step_sin, far_r, far_i = scratch[
            2 * chunks + 3 : 2 * chunks + 9
        ]
        table_sem, own_sem = scratch[2 * chunks + 9 :]

        def table_copies(tile):
            pairs = (base_c, base_cos), (base_s, base_sin), (step_c, step_cos), (step_s, step_sin)
            return [
                pltpu.make_async_copy(
                    source.at[tile, pl.ds(0, mixed)], target.at[tile], table_sem.at[tile, i]
                )
                for i, (source, target) in enumerate(pairs)
            ]

        def own_copies(tile):
            return [
                pltpu.make_async_copy(source.at[tile], target.at[tile], own_sem.at[tile, i])
                for i, (source, target) in enumerate(((own_r, far_r), (own_i, far_i)))
            ]

        for tile in range(tiles):
            for copy in table_copies(tile) + own_copies(tile):
                copy.start()

        def project(tile, part):
            project_rows(
                rows_ref, part * chunk, chunk,
                lambda first, size: weight_ref[class_ref[tile], pl.ds(first, size), :],
                proj[2 * part], proj[2 * part + 1], bins, pixels, piece,
            )

        def turn(tile, part, sums):
            for group in range(chunk // 8):
                at = pl.ds(part * chunk + group * 8, 8)

                def put(ref, at=at):
                    def store(lanes, value):
                        ref[at, lanes] = value

                    return store

                sums = turn_rows(
                    proj[2 * part], proj[2 * part + 1], pl.ds(group * 8, 8),
                    base_cos[tile, at, :], base_sin[tile, at, :],
                    step_cos[tile, at, :], step_sin[tile, at, :],
                    put(turned_r), put(turned_i), sums,
                )
            return sums

        def one_tile(tile, _):
            sums = []
            for b in range(blocks):
                for half in range(2):
                    sums.append(sums_ref[tile, half, :, pl.ds(b * LANES, LANES)])
            for copy in table_copies(tile):
                copy.wait()
            for part in range(chunks):
                following = tile
                if part + 1 == chunks:
                    following = jnp.minimum(tile + 1, tiles - 1)
                project(following, (part + 1) % chunks)
                sums = turn(tile, part, sums)
            heavy = []
            for b in range(blocks):
                lanes = pl.ds(b * LANES, LANES)
                real = jnp.sum(sums[2 * b], axis=0, keepdims=True)
                imag = jnp.sum(sums[2 * b + 1], axis=0, keepdims=True)
                image_ref[tile, 0:1, lanes] = real
                image_ref[tile, 1:2, lanes] = imag
                intensity = real * real + imag * imag
                heavy.append(jnp.broadcast_to(intensity * real, (8, LANES)))
                heavy.append(jnp.broadcast_to(intensity * imag, (8, LANES)))
            for copy in own_copies(tile):
                copy.wait()

            def pull(i, _, real_of, imag_of, first):
                row = pl.multiple_of(i * 8, 8)
                at = pl.ds(pl.multiple_of(first + i * 8, 8), 8)
                total = corr_acc[at, :]
                for b in range(blocks):
                    lanes = pl.ds(b * LANES, LANES)
                    total = total + (
                        real_of(row, lanes) * heavy[2 * b + 1] - imag_of(row, lanes) * heavy[2 * b]
                    )
                corr_acc[at, :] = total
                return 0

            near = functools.partial(
                pull,
                real_of=lambda row, lanes: turned_r[pl.ds(row, 8), lanes],
                imag_of=lambda row, lanes: turned_i[pl.ds(row, 8), lanes],
                first=0,
            )
            far = functools.partial(
                pull,
                real_of=lambda row, lanes: far_r[tile, pl.ds(row, 8), lanes],
                imag_of=lambda row, lanes: far_i[tile, pl.ds(row, 8), lanes],
                first=mixed,
            )
            lax.fori_loop(0, mixed // 8, near, 0, unroll=4)
            lax.fori_loop(0, own // 8, far, 0, unroll=4)
            return 0

        corr_acc[...] = jnp.zeros_like(corr_acc)
        project(0, 0)
        lax.fori_loop(0, tiles, one_tile, 0)
        for part in range((mixed + own) // LANES):
            block = corr_acc[pl.ds(part * LANES, LANES), :]
            corr_ref[pl.ds(part, 1), :] = jnp.sum(block.T, axis=0, keepdims=True)

    return focus_kernel


def focus(tile_class, arrived, weight_tiles, tables, own_parts, chunk, piece):
    turned_own_r, turned_own_i, own_sums = own_parts
    mixed, _ = arrived.shape
    own = turned_own_r.shape[1]
    slots = mixed + own
    _, pixels, bins = weight_tiles.shape
    tiles = tile_class.shape[0]
    vmem = pl.BlockSpec(memory_space=pltpu.VMEM)
    hbm = pl.BlockSpec(memory_space=pltpu.HBM)
    image, corr = pl.pallas_call(
        make_focus_kernel(mixed, own, pixels, bins, tiles, chunk, piece),
        in_specs=[pl.BlockSpec(memory_space=pltpu.SMEM), vmem, vmem, vmem] + [hbm] * 6,
        out_specs=[vmem] * 2,
        scratch_shapes=[pltpu.VMEM((chunk, pixels), jnp.float32)] * (2 * (mixed // chunk))
        + [
            pltpu.VMEM((mixed, pixels), jnp.float32),
            pltpu.VMEM((mixed, pixels), jnp.float32),
            pltpu.VMEM((slots, LANES), jnp.float32),
        ]
        + [pltpu.VMEM((tiles, mixed, LANES), jnp.float32)] * 4
        + [pltpu.VMEM((tiles, own, pixels), jnp.float32)] * 2
        + [
            pltpu.SemaphoreType.DMA((tiles, 4)),
            pltpu.SemaphoreType.DMA((tiles, 2)),
        ],
        out_shape=[
            jax.ShapeDtypeStruct((tiles, 2, pixels), jnp.float32),
            jax.ShapeDtypeStruct((slots // LANES, LANES), jnp.float32),
        ],
        compiler_params=pltpu.CompilerParams(vmem_limit_bytes=ALL_VMEM),
        name="focus",
    )(tile_class, arrived, own_sums, weight_tiles, *tables, turned_own_r, turned_own_i)
    return image, corr.reshape(slots)


def on_device(
    panels, phases, weight_tiles, tile_class, send_slots, foot_slot, foot_ping, tile_counts
):
    track_devs = lax.axis_size("track")
    tile_devs = lax.axis_size("tile")
    device = lax.axis_index("track") * tile_devs + lax.axis_index("tile")
    ping_local = phases.shape[0]
    row_width = panels.shape[1]
    tiles_here = tile_counts.shape[0]
    pixels = weight_tiles.shape[1]
    slots = send_slots.shape[0]
    slot_cap = slots // 3 // tile_devs
    ping_total = ping_local * track_devs * tile_devs
    tile_total = tiles_here * track_devs * tile_devs

    blocks = (tile_devs, slot_cap, row_width)
    group = slots // 3
    (own,) = gather_rotated(panels, phases, send_slots, (1,))
    own_arrived = lax.all_to_all(
        own.reshape(blocks), "tile", split_axis=0, concat_axis=0, tiled=True
    )
    to_next, to_last = gather_rotated(panels, phases, send_slots, (2, 0))
    behind = shift_along(to_next.reshape(blocks), "track", 1)
    ahead = shift_along(to_last.reshape(blocks), "track", -1)
    mixed = jnp.concatenate([behind, ahead], axis=1)
    mixed, own_arrived = lax.optimization_barrier((mixed, own_arrived))
    arrived = lax.all_to_all(mixed, "tile", split_axis=0, concat_axis=0, tiled=True)
    tables = phase_tables(
        (device * tiles_here).astype(jnp.int32).reshape(1),
        tile_counts, foot_slot, foot_ping, slots,
        ping_total, tile_total, track_devs, tile_devs, pixels,
    )
    own_parts = own_forward(
        tile_class, own_arrived.reshape(group, row_width), weight_tiles, tables, 2 * group
    )
    image, corr = focus(
        tile_class, arrived.reshape(2 * group, row_width), weight_tiles, tables, own_parts, group, 256
    )

    mixed_corr = corr[: 2 * group].reshape(tile_devs, 2, slot_cap)
    own_corr = corr[2 * group :].reshape(tile_devs, slot_cap)
    track = lax.axis_index("track")
    spread = jnp.zeros((track_devs + 2, tile_devs, slot_cap), jnp.float32)
    spread = lax.dynamic_update_slice_in_dim(
        spread, jnp.stack([mixed_corr[:, 0], own_corr, mixed_corr[:, 1]]), track, 0
    )
    spread = spread[1 : track_devs + 1].reshape(track_devs * tile_devs, slot_cap)
    back = lax.all_to_all(spread, ("track", "tile"), split_axis=0, concat_axis=0, tiled=True)
    back = jnp.pad(back.reshape(track_devs, tile_devs, slot_cap), ((1, 1), (0, 0), (0, 0)))
    back = lax.dynamic_slice_in_dim(back, track, 3, 0).reshape(1, slots)
    owner = (send_slots // (panels.shape[0] // ping_local)).reshape(1, slots)
    mine = lax.broadcasted_iota(jnp.int32, (ping_local, slots), 0) == owner
    ping_gradient = jnp.sum(jnp.where(mine & (send_slots >= 0)[None, :], back, 0.0), axis=1)
    return (image, ping_gradient)


def solution(mesh):
    spread = P(("track", "tile"))
    in_specs = (
        P(("track", "tile"), None), spread, P(), spread, spread,
        P(("track", "tile"), None), P(("track", "tile"), None), spread,
    )
    out_specs = (P(("track", "tile"), None, None), spread)
    return jax.shard_map(
        on_device, mesh=mesh, in_specs=in_specs, out_specs=out_specs, check_vma=False
    )
```

```python
import functools
import math

import jax
import jax.numpy as jnp
from jax import lax
from jax.experimental import pallas as pl
from jax.experimental.pallas import tpu as pltpu
from jax.sharding import PartitionSpec as P

LANES = 128
HALF = 128
ALL_VMEM = 60 * 1024 * 1024


def shift_along(block, axis, distance):
    devices = range(lax.axis_size(axis))
    route = [(i - distance, i) for i in devices if i - distance in devices]
    return lax.ppermute(block, axis, route)


def whole(shape):
    return pl.BlockSpec(shape, lambda *_: (0,) * len(shape))


def column(row):
    return jnp.broadcast_to(row, (8, row.shape[1])).T[:, :1]


def rotated_rows(panels_ref, phases_ref, slots_ref, first, count):
    rows_here, width = panels_ref.shape
    bins = width // 2
    pings = phases_ref.shape[1]
    columns = [
        column(slots_ref[pl.ds(row, 1), :].astype(jnp.float32))
        for row in range(first // LANES, (first + count) // LANES)
    ]
    slot_row = jnp.concatenate(columns, axis=0).astype(jnp.int32)
    row_ids = lax.broadcasted_iota(jnp.int32, (count, rows_here), 1)
    pick = jnp.where(row_ids == slot_row, 1.0, 0.0).astype(jnp.bfloat16)
    picked = jnp.dot(pick, panels_ref[...], preferred_element_type=jnp.float32)
    phases = phases_ref[...]
    ping_ids = lax.broadcasted_iota(jnp.int32, (count, pings), 1)
    owned = ping_ids == (slot_row // (rows_here // pings))
    cos_col = jnp.sum(jnp.where(owned, jnp.cos(phases), 0.0), axis=1, keepdims=True)
    sin_col = jnp.sum(jnp.where(owned, jnp.sin(phases), 0.0), axis=1, keepdims=True)
    real_part = picked[:, :bins]
    imag_part = picked[:, bins:]
    return (
        (cos_col * real_part - sin_col * imag_part).astype(jnp.bfloat16),
        (sin_col * real_part + cos_col * imag_part).astype(jnp.bfloat16),
    )


def gather_rotated(panels, phases, slots, offsets):
    count = slots.shape[0] // 3
    width = panels.shape[1]
    bins = width // 2

    def kernel(panels_ref, phases_ref, slots_ref, *outs):
        for offset, out in zip(offsets, outs):
            real_part, imag_part = rotated_rows(
                panels_ref, phases_ref, slots_ref, offset * count, count
            )
            out[:, :bins] = real_part
            out[:, bins:] = imag_part

    return pl.pallas_call(
        kernel,
        out_shape=[jax.ShapeDtypeStruct((count, width), jnp.bfloat16) for _ in offsets],
        compiler_params=pltpu.CompilerParams(vmem_limit_bytes=ALL_VMEM),
        name="gather_rotated",
    )(panels, phases.reshape(1, -1), slots.reshape(-1, LANES))


def cos_sin(angle):
    turns = jnp.round(angle * (2.0 / math.pi))
    rest = angle - turns * 1.5703125
    rest = rest - turns * 4.837512969970703125e-4
    rest = rest - turns * 7.549789948768648e-8
    square = rest * rest
    sine = (-1.9515295891e-4 * square + 8.3321608736e-3) * square - 1.6666654611e-1
    sine = sine * square * rest + rest
    cosine = (2.443315711809948e-5 * square - 1.388731625493765e-3) * square
    cosine = (cosine + 4.166664568298827e-2) * square * square - 0.5 * square + 1.0
    quarter = turns.astype(jnp.int32)
    odd = (quarter & 1) == 1
    cos_out = jnp.where(odd, sine, cosine)
    sin_out = jnp.where(odd, cosine, sine)
    cos_out = jnp.where(((quarter + 1) & 2) == 2, -cos_out, cos_out)
    sin_out = jnp.where((quarter & 2) == 2, -sin_out, sin_out)
    return cos_out, sin_out


def make_table_kernel(ping_total, tile_total, track_groups, pixels, tile_devs, slots, tiles):
    def table_kernel(base_ref, counts_ref, slot_ref, ping_ref, base_cos, base_sin, step_cos, step_sin):
        foot = slot_ref.shape[1]
        group = slots // 3
        cap = group // tile_devs
        slot_ids = lax.broadcasted_iota(jnp.int32, (slots, foot), 0)
        lane = lax.broadcasted_iota(jnp.int32, (1, LANES), 1)
        across = (lane.astype(jnp.float32) + 0.5) / pixels - 0.5
        step_angle = jnp.zeros((slots, LANES), jnp.float32)
        for tile in range(tiles):
            listed = slot_ref[tile : tile + 1, :]
            offset = listed // group
            source = (listed % group) // cap
            place = listed % cap
            placed = jnp.where(
                offset == 1,
                2 * group + source * cap + place,
                (source * 2 + offset // 2) * cap + place,
            )
            match = jnp.where(slot_ids == placed, 1.0, 0.0).astype(jnp.bfloat16)
            pings = ping_ref[tile : tile + 1, :]
            entry = lax.broadcasted_iota(jnp.int32, (1, foot), 1)
            used = jnp.where(entry < counts_ref[tile], 1.0, 0.0)
            values = jnp.concatenate(
                [
                    (pings // HALF).astype(jnp.float32) * used,
                    (pings % HALF).astype(jnp.float32) * used,
                    used,
                    jnp.zeros((5, foot), jnp.float32),
                ],
                axis=0,
            ).astype(jnp.bfloat16)
            found = lax.dot_general(
                match, values, (((1,), (1,)), ((), ())), preferred_element_type=jnp.float32
            )
            ping = (found[:, 0:1] * HALF + found[:, 1:2]).astype(jnp.int32)
            mask = found[:, 2:3]
            gap = (2 * ping + 1) * tile_total - (2 * (base_ref[0] + tile) + 1) * ping_total
            along = gap.astype(jnp.float32) * (track_groups / (2.0 * ping_total * tile_total))
            cosine, sine = cos_sin(96.0 * across * along + 8.0 * (along * along))
            base_cos[tile] = cosine * mask
            base_sin[tile] = sine * mask
            step_angle = jnp.where(lane == tile, (96.0 * LANES / pixels) * along, step_angle)
        cosine, sine = cos_sin(step_angle)
        for tile in range(tiles):
            step_cos[tile] = jnp.broadcast_to(cosine[:, tile : tile + 1], (slots, LANES))
            step_sin[tile] = jnp.broadcast_to(sine[:, tile : tile + 1], (slots, LANES))

    return table_kernel


def phase_tables(
    base, counts, foot_slot, foot_ping, slots, ping_total, tile_total, track_groups, tile_devs, pixels
):
    tiles, foot = foot_slot.shape
    kernel = make_table_kernel(ping_total, tile_total, track_groups, pixels, tile_devs, slots, tiles)
    table = jax.ShapeDtypeStruct((tiles, slots, LANES), jnp.float32)
    smem = pl.BlockSpec(memory_space=pltpu.SMEM)
    vmem = pl.BlockSpec(memory_space=pltpu.VMEM)
    return pl.pallas_call(
        kernel,
        in_specs=[smem, smem, vmem, vmem],
        out_specs=[vmem] * 4,
        out_shape=[table] * 4,
        compiler_params=pltpu.CompilerParams(vmem_limit_bytes=ALL_VMEM),
        name="phase_tables",
    )(base, counts, foot_slot, foot_ping)


def turn_rows(real_ref, imag_ref, rows, cos_now, sin_now, turn_c, turn_s, out_r, out_i, sums):
    blocks = len(sums) // 2
    sums = list(sums)
    for b in range(blocks):
        lanes = pl.ds(b * LANES, LANES)
        real = real_ref[rows, lanes]
        imag = imag_ref[rows, lanes]
        new_r = cos_now * real - sin_now * imag
        new_i = sin_now * real + cos_now * imag
        out_r(lanes, new_r)
        out_i(lanes, new_i)
        sums[2 * b] = sums[2 * b] + new_r
        sums[2 * b + 1] = sums[2 * b + 1] + new_i
        if b + 1 < blocks:
            cos_now, sin_now = (
                cos_now * turn_c - sin_now * turn_s,
                sin_now * turn_c + cos_now * turn_s,
            )
    return sums


def project_rows(rows_ref, first_row, count, weight, out_r, out_i, bins, pixels, piece):
    for first in range(0, pixels, piece):
        for half, out in enumerate((out_r, out_i)):
            out[:, pl.ds(first, piece)] = lax.dot_general(
                rows_ref[pl.ds(first_row, count), pl.ds(half * bins, bins)],
                weight(first, piece),
                (((1,), (1,)), ((), ())),
                preferred_element_type=jnp.float32,
            )


def own_forward(tile_class, own, weight_tiles, tables, first_slot):
    count, width = own.shape
    _, pixels, bins = weight_tiles.shape
    tiles = tile_class.shape[0]
    blocks = pixels // LANES
    block_at = first_slot // count

    def kernel(class_ref, rows_ref, weight_ref, base_c, base_s, step_c, step_s, turned_r, turned_i, proj_r, proj_i):
        project_rows(
            rows_ref, 0, count, lambda first, size: weight_ref[0, pl.ds(first, size), :],
            proj_r, proj_i, bins, pixels, pixels,
        )

        def group(i, sums):
            at = pl.ds(pl.multiple_of(i * 8, 8), 8)

            def put(ref):
                def store(lanes, value):
                    ref[0, at, lanes] = value

                return store

            return tuple(
                turn_rows(
                    proj_r, proj_i, at, base_c[0, at, :], base_s[0, at, :], step_c[0, at, :],
                    step_s[0, at, :], put(turned_r), put(turned_i), sums,
                )
            )

        sums = (jnp.zeros((8, LANES), jnp.float32),) * (2 * blocks)
        sums = lax.fori_loop(0, count // 8, group, sums, unroll=4)
        for b in range(blocks):
            for half in range(2):
                total = jnp.sum(sums[2 * b + half], axis=0, keepdims=True)
                store = turned_i if half else turned_r
                store[0, pl.ds(count, 8), pl.ds(b * LANES, LANES)] = jnp.broadcast_to(total, (8, LANES))

    table_spec = pl.BlockSpec((1, count, LANES), lambda t, *_: (t, block_at, 0))
    turned = jax.ShapeDtypeStruct((tiles, count + 8, pixels), jnp.float32)
    turned_spec = pl.BlockSpec((1, count + 8, pixels), lambda t, *_: (t, 0, 0))
    return pl.pallas_call(
        kernel,
        grid_spec=pltpu.PrefetchScalarGridSpec(
            num_scalar_prefetch=1,
            grid=(tiles,),
            in_specs=[
                pl.BlockSpec((count, width), lambda t, *_: (0, 0)),
                pl.BlockSpec((1, pixels, bins), lambda t, cls: (cls[t], 0, 0)),
            ]
            + [table_spec] * 4,
            out_specs=[turned_spec, turned_spec],
            scratch_shapes=[pltpu.VMEM((count, pixels), jnp.float32)] * 2,
        ),
        out_shape=[turned, turned],
        compiler_params=pltpu.CompilerParams(vmem_limit_bytes=ALL_VMEM),
        name="own_forward",
    )(tile_class, own, weight_tiles, *tables)


def make_focus_kernel(mixed, own, pixels, bins, tiles, chunk, piece, tracks, cap):
    blocks = pixels // LANES
    chunks = mixed // chunk

    def focus_kernel(
        class_ref, track_ref, rows_ref, weight_ref, base_c, base_s, step_c, step_s, own_r, own_i,
        image_ref, corr_ref, *scratch,
    ):
        proj = scratch[: 2 * chunks]
        turned_r, turned_i, corr_acc = scratch[2 * chunks : 2 * chunks + 3]
        base_cos, base_sin, step_cos, step_sin, far_r, far_i = scratch[
            2 * chunks + 3 : 2 * chunks + 9
        ]
        table_sem, own_sem = scratch[2 * chunks + 9 :]

        def table_copies(tile):
            pairs = (base_c, base_cos), (base_s, base_sin), (step_c, step_cos), (step_s, step_sin)
            return [
                pltpu.make_async_copy(
                    source.at[tile, pl.ds(0, mixed)], target.at[tile], table_sem.at[tile, i]
                )
                for i, (source, target) in enumerate(pairs)
            ]

        def own_copies(tile):
            return [
                pltpu.make_async_copy(source.at[tile], target.at[tile], own_sem.at[tile, i])
                for i, (source, target) in enumerate(((own_r, far_r), (own_i, far_i)))
            ]

        for tile in range(tiles):
            for copy in table_copies(tile) + own_copies(tile):
                copy.start()

        pieces = 2 * (pixels // piece)

        def project(tile, part, low, high):
            for index in range(low, high):
                first, half = (index // 2) * piece, index % 2
                proj[2 * part + half][:, pl.ds(first, piece)] = lax.dot_general(
                    rows_ref[pl.ds(part * chunk, chunk), pl.ds(half * bins, bins)],
                    weight_ref[class_ref[tile], pl.ds(first, piece), :],
                    (((1,), (1,)), ((), ())),
                    preferred_element_type=jnp.float32,
                )

        def turn(tile, part, sums):
            for group in range(chunk // 8):
                at = pl.ds(part * chunk + group * 8, 8)

                def put(ref, at=at):
                    def store(lanes, value):
                        ref[at, lanes] = value

                    return store

                sums = turn_rows(
                    proj[2 * part], proj[2 * part + 1], pl.ds(group * 8, 8),
                    base_cos[tile, at, :], base_sin[tile, at, :],
                    step_cos[tile, at, :], step_sin[tile, at, :],
                    put(turned_r), put(turned_i), sums,
                )
            return sums

        def one_tile(tile, _):
            sums = [jnp.zeros((8, LANES), jnp.float32)] * (2 * blocks)
            for copy in table_copies(tile):
                copy.wait()
            for part in range(chunks):
                last = part + 1 == chunks
                following = jnp.minimum(tile + 1, tiles - 1) if last else tile
                project(following, (part + 1) % chunks, 0, pieces)
                sums = turn(tile, part, sums)
            for copy in own_copies(tile):
                copy.wait()
            heavy = []
            for b in range(blocks):
                lanes = pl.ds(b * LANES, LANES)
                real = far_r[tile, own : own + 1, lanes] + jnp.sum(sums[2 * b], axis=0, keepdims=True)
                imag = far_i[tile, own : own + 1, lanes] + jnp.sum(sums[2 * b + 1], axis=0, keepdims=True)
                image_ref[tile, 0:1, lanes] = real
                image_ref[tile, 1:2, lanes] = imag
                intensity = real * real + imag * imag
                heavy.append(jnp.broadcast_to(intensity * real, (8, LANES)))
                heavy.append(jnp.broadcast_to(intensity * imag, (8, LANES)))
            for group in range((mixed + own) // 8):
                at = pl.ds(group * 8, 8)
                total = corr_acc[at, :]
                for b in range(blocks):
                    lanes = pl.ds(b * LANES, LANES)
                    if group * 8 < mixed:
                        real, imag = turned_r[at, lanes], turned_i[at, lanes]
                    else:
                        near = pl.ds(group * 8 - mixed, 8)
                        real, imag = far_r[tile, near, lanes], far_i[tile, near, lanes]
                    total = total + (real * heavy[2 * b + 1] - imag * heavy[2 * b])
                corr_acc[at, :] = total
            return 0

        corr_acc[...] = jnp.zeros_like(corr_acc)
        project(0, 0, 0, pieces)
        lax.fori_loop(0, tiles, one_tile, 0)
        totals = jnp.sum(corr_acc[...], axis=1, keepdims=True)
        row = lax.broadcasted_iota(jnp.int32, (mixed + own, LANES), 0)
        lane = lax.broadcasted_iota(jnp.int32, (mixed + own, LANES), 1)
        placed = jnp.where(row % cap == lane, totals, 0.0)
        placed = jnp.sum(placed.reshape((mixed + own) // cap, cap, LANES), axis=1)
        corr_acc[pl.ds(0, (mixed + own) // cap), :] = placed
        corr_ref[...] = jnp.zeros_like(corr_ref)
        track = track_ref[0]
        sources = own // cap
        cuts = (pl.ds(0, sources, stride=2), pl.ds(2 * sources, sources), pl.ds(1, sources, stride=2))
        for k, cut in enumerate(cuts):

            @pl.when((track + k >= 1) & (track + k <= tracks))
            def _(k=k, cut=cut):
                target = pl.ds(pl.multiple_of((track + k - 1) * sources, sources), sources)
                corr_ref[target, :] = corr_acc[cut, :][:, :cap]

    return focus_kernel


def focus(tile_class, track, arrived, weight_tiles, tables, own_parts, chunk, piece, tracks, cap):
    turned_own_r, turned_own_i = own_parts
    mixed, _ = arrived.shape
    own = turned_own_r.shape[1] - 8
    slots = mixed + own
    _, pixels, bins = weight_tiles.shape
    tiles = tile_class.shape[0]
    vmem = pl.BlockSpec(memory_space=pltpu.VMEM)
    hbm = pl.BlockSpec(memory_space=pltpu.HBM)
    image, corr = pl.pallas_call(
        make_focus_kernel(mixed, own, pixels, bins, tiles, chunk, piece, tracks, cap),
        in_specs=[pl.BlockSpec(memory_space=pltpu.SMEM)] * 2 + [vmem] * 2 + [hbm] * 6,
        out_specs=[vmem] * 2,
        scratch_shapes=[pltpu.VMEM((chunk, pixels), jnp.float32)] * (2 * (mixed // chunk))
        + [
            pltpu.VMEM((mixed, pixels), jnp.float32),
            pltpu.VMEM((mixed, pixels), jnp.float32),
            pltpu.VMEM((slots, LANES), jnp.float32),
        ]
        + [pltpu.VMEM((tiles, mixed, LANES), jnp.float32)] * 4
        + [pltpu.VMEM((tiles, own + 8, pixels), jnp.float32)] * 2
        + [
            pltpu.SemaphoreType.DMA((tiles, 4)),
            pltpu.SemaphoreType.DMA((tiles, 2)),
        ],
        out_shape=[
            jax.ShapeDtypeStruct((tiles, 2, pixels), jnp.float32),
            jax.ShapeDtypeStruct((tracks * own // cap, cap), jnp.float32),
        ],
        compiler_params=pltpu.CompilerParams(vmem_limit_bytes=52 * 1024 * 1024),
        name="focus",
    )(tile_class, track, arrived, weight_tiles, *tables, turned_own_r, turned_own_i)
    return image, corr


def on_device(
    panels, phases, weight_tiles, tile_class, send_slots, foot_slot, foot_ping, tile_counts
):
    track_devs = lax.axis_size("track")
    tile_devs = lax.axis_size("tile")
    device = lax.axis_index("track") * tile_devs + lax.axis_index("tile")
    ping_local = phases.shape[0]
    row_width = panels.shape[1]
    tiles_here = tile_counts.shape[0]
    pixels = weight_tiles.shape[1]
    slots = send_slots.shape[0]
    slot_cap = slots // 3 // tile_devs
    ping_total = ping_local * track_devs * tile_devs
    tile_total = tiles_here * track_devs * tile_devs

    blocks = (tile_devs, slot_cap, row_width)
    group = slots // 3
    (own,) = gather_rotated(panels, phases, send_slots, (1,))
    own_arrived = lax.all_to_all(
        own.reshape(blocks), "tile", split_axis=0, concat_axis=0, tiled=True
    )
    to_next, to_last = gather_rotated(panels, phases, send_slots, (2, 0))
    behind = shift_along(to_next.reshape(blocks), "track", 1)
    ahead = shift_along(to_last.reshape(blocks), "track", -1)
    mixed = jnp.concatenate([behind, ahead], axis=1)
    mixed, own_arrived = lax.optimization_barrier((mixed, own_arrived))
    arrived = lax.all_to_all(mixed, "tile", split_axis=0, concat_axis=0, tiled=True)
    tables = phase_tables(
        (device * tiles_here).astype(jnp.int32).reshape(1),
        tile_counts, foot_slot, foot_ping, slots,
        ping_total, tile_total, track_devs, tile_devs, pixels,
    )
    own_parts = own_forward(
        tile_class, own_arrived.reshape(group, row_width), weight_tiles, tables, 2 * group
    )
    track = lax.axis_index("track")
    image, corr = focus(
        tile_class, track.astype(jnp.int32).reshape(1), arrived.reshape(2 * group, row_width),
        weight_tiles, tables, own_parts, group, 256, track_devs, slot_cap,
    )
    back = lax.all_to_all(corr, ("track", "tile"), split_axis=0, concat_axis=0, tiled=True)
    back = jnp.pad(back.reshape(track_devs, tile_devs, slot_cap), ((1, 1), (0, 0), (0, 0)))
    back = lax.dynamic_slice_in_dim(back, track, 3, 0).reshape(1, slots)
    owner = (send_slots // (panels.shape[0] // ping_local)).reshape(1, slots)
    mine = lax.broadcasted_iota(jnp.int32, (ping_local, slots), 0) == owner
    ping_gradient = jnp.sum(jnp.where(mine & (send_slots >= 0)[None, :], back, 0.0), axis=1)
    return (image, ping_gradient)


def solution(mesh):
    spread = P(("track", "tile"))
    in_specs = (
        P(("track", "tile"), None), spread, P(), spread, spread,
        P(("track", "tile"), None), P(("track", "tile"), None), spread,
    )
    out_specs = (P(("track", "tile"), None, None), spread)
    return jax.shard_map(
        on_device, mesh=mesh, in_specs=in_specs, out_specs=out_specs, check_vma=False
    )
```

```python
import functools
import math

import jax
import jax.numpy as jnp
from jax import lax
from jax.experimental import pallas as pl
from jax.experimental.pallas import tpu as pltpu
from jax.sharding import PartitionSpec as P

LANES = 128
HALF = 128
ALL_VMEM = 60 * 1024 * 1024


def shift_along(block, axis, distance):
    devices = range(lax.axis_size(axis))
    route = [(i - distance, i) for i in devices if i - distance in devices]
    return lax.ppermute(block, axis, route)


def whole(shape):
    return pl.BlockSpec(shape, lambda *_: (0,) * len(shape))


def column(row):
    return jnp.broadcast_to(row, (8, row.shape[1])).T[:, :1]


def rotated_rows(panels_ref, phases_ref, slots_ref, first, count):
    rows_here, width = panels_ref.shape
    bins = width // 2
    pings = phases_ref.shape[1]
    columns = [
        column(slots_ref[pl.ds(row, 1), :].astype(jnp.float32))
        for row in range(first // LANES, (first + count) // LANES)
    ]
    slot_row = jnp.concatenate(columns, axis=0).astype(jnp.int32)
    row_ids = lax.broadcasted_iota(jnp.int32, (count, rows_here), 1)
    pick = jnp.where(row_ids == slot_row, 1.0, 0.0).astype(jnp.bfloat16)
    picked = jnp.dot(pick, panels_ref[...], preferred_element_type=jnp.float32)
    phases = phases_ref[...]
    ping_ids = lax.broadcasted_iota(jnp.int32, (count, pings), 1)
    owned = ping_ids == (slot_row // (rows_here // pings))
    cos_col = jnp.sum(jnp.where(owned, jnp.cos(phases), 0.0), axis=1, keepdims=True)
    sin_col = jnp.sum(jnp.where(owned, jnp.sin(phases), 0.0), axis=1, keepdims=True)
    real_part = picked[:, :bins]
    imag_part = picked[:, bins:]
    return (
        (cos_col * real_part - sin_col * imag_part).astype(jnp.bfloat16),
        (sin_col * real_part + cos_col * imag_part).astype(jnp.bfloat16),
    )


def gather_rotated(panels, phases, slots, offsets):
    count = slots.shape[0] // 3
    width = panels.shape[1]
    bins = width // 2

    def kernel(panels_ref, phases_ref, slots_ref, *outs):
        for offset, out in zip(offsets, outs):
            real_part, imag_part = rotated_rows(
                panels_ref, phases_ref, slots_ref, offset * count, count
            )
            out[:, :bins] = real_part
            out[:, bins:] = imag_part

    return pl.pallas_call(
        kernel,
        out_shape=[jax.ShapeDtypeStruct((count, width), jnp.bfloat16) for _ in offsets],
        compiler_params=pltpu.CompilerParams(vmem_limit_bytes=ALL_VMEM),
        name="gather_rotated",
    )(panels, phases.reshape(1, -1), slots.reshape(-1, LANES))


def cos_sin(angle):
    turns = jnp.round(angle * (2.0 / math.pi))
    rest = angle - turns * 1.5703125
    rest = rest - turns * 4.837512969970703125e-4
    rest = rest - turns * 7.549789948768648e-8
    square = rest * rest
    sine = (-1.9515295891e-4 * square + 8.3321608736e-3) * square - 1.6666654611e-1
    sine = sine * square * rest + rest
    cosine = (2.443315711809948e-5 * square - 1.388731625493765e-3) * square
    cosine = (cosine + 4.166664568298827e-2) * square * square - 0.5 * square + 1.0
    quarter = turns.astype(jnp.int32)
    odd = (quarter & 1) == 1
    cos_out = jnp.where(odd, sine, cosine)
    sin_out = jnp.where(odd, cosine, sine)
    cos_out = jnp.where(((quarter + 1) & 2) == 2, -cos_out, cos_out)
    sin_out = jnp.where((quarter & 2) == 2, -sin_out, sin_out)
    return cos_out, sin_out


def make_table_kernel(ping_total, tile_total, track_groups, pixels, tile_devs, slots, tiles):
    def table_kernel(base_ref, counts_ref, slot_ref, ping_ref, base_cos, base_sin, step_cos, step_sin):
        foot = slot_ref.shape[1]
        group = slots // 3
        cap = group // tile_devs
        slot_ids = lax.broadcasted_iota(jnp.int32, (slots, foot), 0)
        lane = lax.broadcasted_iota(jnp.int32, (1, LANES), 1)
        across = (lane.astype(jnp.float32) + 0.5) / pixels - 0.5
        step_angle = jnp.zeros((slots, LANES), jnp.float32)
        for tile in range(tiles):
            listed = slot_ref[tile : tile + 1, :]
            offset = listed // group
            source = (listed % group) // cap
            place = listed % cap
            placed = jnp.where(
                offset == 1,
                2 * group + source * cap + place,
                (source * 2 + offset // 2) * cap + place,
            )
            match = jnp.where(slot_ids == placed, 1.0, 0.0).astype(jnp.bfloat16)
            pings = ping_ref[tile : tile + 1, :]
            entry = lax.broadcasted_iota(jnp.int32, (1, foot), 1)
            used = jnp.where(entry < counts_ref[tile], 1.0, 0.0)
            values = jnp.concatenate(
                [
                    (pings // HALF).astype(jnp.float32) * used,
                    (pings % HALF).astype(jnp.float32) * used,
                    used,
                    jnp.zeros((5, foot), jnp.float32),
                ],
                axis=0,
            ).astype(jnp.bfloat16)
            found = lax.dot_general(
                match, values, (((1,), (1,)), ((), ())), preferred_element_type=jnp.float32
            )
            ping = (found[:, 0:1] * HALF + found[:, 1:2]).astype(jnp.int32)
            mask = found[:, 2:3]
            gap = (2 * ping + 1) * tile_total - (2 * (base_ref[0] + tile) + 1) * ping_total
            along = gap.astype(jnp.float32) * (track_groups / (2.0 * ping_total * tile_total))
            cosine, sine = cos_sin(96.0 * across * along + 8.0 * (along * along))
            base_cos[tile] = cosine * mask
            base_sin[tile] = sine * mask
            step_angle = jnp.where(lane == tile, (96.0 * LANES / pixels) * along, step_angle)
        cosine, sine = cos_sin(step_angle)
        for tile in range(tiles):
            step_cos[tile] = jnp.broadcast_to(cosine[:, tile : tile + 1], (slots, LANES))
            step_sin[tile] = jnp.broadcast_to(sine[:, tile : tile + 1], (slots, LANES))

    return table_kernel


def phase_tables(
    base, counts, foot_slot, foot_ping, slots, ping_total, tile_total, track_groups, tile_devs, pixels
):
    tiles, foot = foot_slot.shape
    kernel = make_table_kernel(ping_total, tile_total, track_groups, pixels, tile_devs, slots, tiles)
    table = jax.ShapeDtypeStruct((tiles, slots, LANES), jnp.float32)
    smem = pl.BlockSpec(memory_space=pltpu.SMEM)
    vmem = pl.BlockSpec(memory_space=pltpu.VMEM)
    return pl.pallas_call(
        kernel,
        in_specs=[smem, smem, vmem, vmem],
        out_specs=[vmem] * 4,
        out_shape=[table] * 4,
        compiler_params=pltpu.CompilerParams(vmem_limit_bytes=ALL_VMEM),
        name="phase_tables",
    )(base, counts, foot_slot, foot_ping)


def turn_rows(real_ref, imag_ref, rows, cos_now, sin_now, turn_c, turn_s, out_r, out_i, sums):
    blocks = len(sums) // 2
    sums = list(sums)
    for b in range(blocks):
        lanes = pl.ds(b * LANES, LANES)
        real = real_ref[rows, lanes]
        imag = imag_ref[rows, lanes]
        new_r = cos_now * real - sin_now * imag
        new_i = sin_now * real + cos_now * imag
        out_r(lanes, new_r)
        out_i(lanes, new_i)
        sums[2 * b] = sums[2 * b] + new_r
        sums[2 * b + 1] = sums[2 * b + 1] + new_i
        if b + 1 < blocks:
            cos_now, sin_now = (
                cos_now * turn_c - sin_now * turn_s,
                sin_now * turn_c + cos_now * turn_s,
            )
    return sums


def project_rows(rows_ref, first_row, count, weight, out_r, out_i, bins, pixels, piece):
    for first in range(0, pixels, piece):
        for half, out in enumerate((out_r, out_i)):
            out[:, pl.ds(first, piece)] = lax.dot_general(
                rows_ref[pl.ds(first_row, count), pl.ds(half * bins, bins)],
                weight(first, piece),
                (((1,), (1,)), ((), ())),
                preferred_element_type=jnp.float32,
            )


def own_forward(tile_class, own, weight_tiles, tables, first_slot):
    count, width = own.shape
    _, pixels, bins = weight_tiles.shape
    tiles = tile_class.shape[0]
    blocks = pixels // LANES
    block_at = first_slot // count

    def kernel(class_ref, rows_ref, weight_ref, base_c, base_s, step_c, step_s, turned_r, turned_i, proj_r, proj_i):
        project_rows(
            rows_ref, 0, count, lambda first, size: weight_ref[0, pl.ds(first, size), :],
            proj_r, proj_i, bins, pixels, pixels,
        )

        def group(i, sums):
            at = pl.ds(pl.multiple_of(i * 8, 8), 8)

            def put(ref):
                def store(lanes, value):
                    ref[0, at, lanes] = value

                return store

            return tuple(
                turn_rows(
                    proj_r, proj_i, at, base_c[0, at, :], base_s[0, at, :], step_c[0, at, :],
                    step_s[0, at, :], put(turned_r), put(turned_i), sums,
                )
            )

        sums = (jnp.zeros((8, LANES), jnp.float32),) * (2 * blocks)
        sums = lax.fori_loop(0, count // 8, group, sums, unroll=4)
        for b in range(blocks):
            for half in range(2):
                total = jnp.sum(sums[2 * b + half], axis=0, keepdims=True)
                store = turned_i if half else turned_r
                store[0, pl.ds(count, 8), pl.ds(b * LANES, LANES)] = jnp.broadcast_to(total, (8, LANES))

    table_spec = pl.BlockSpec((1, count, LANES), lambda t, *_: (t, block_at, 0))
    turned = jax.ShapeDtypeStruct((tiles, count + 8, pixels), jnp.float32)
    turned_spec = pl.BlockSpec((1, count + 8, pixels), lambda t, *_: (t, 0, 0))
    return pl.pallas_call(
        kernel,
        grid_spec=pltpu.PrefetchScalarGridSpec(
            num_scalar_prefetch=1,
            grid=(tiles,),
            in_specs=[
                pl.BlockSpec((count, width), lambda t, *_: (0, 0)),
                pl.BlockSpec((1, pixels, bins), lambda t, cls: (cls[t], 0, 0)),
            ]
            + [table_spec] * 4,
            out_specs=[turned_spec, turned_spec],
            scratch_shapes=[pltpu.VMEM((count, pixels), jnp.float32)] * 2,
        ),
        out_shape=[turned, turned],
        compiler_params=pltpu.CompilerParams(vmem_limit_bytes=ALL_VMEM),
        name="own_forward",
    )(tile_class, own, weight_tiles, *tables)


def make_focus_kernel(mixed, own, pixels, bins, tiles, chunk, piece, tracks, cap):
    blocks = pixels // LANES
    chunks = mixed // chunk

    def focus_kernel(
        class_ref, track_ref, rows_ref, weight_ref, base_c, base_s, step_c, step_s, own_r, own_i,
        image_ref, corr_ref, *scratch,
    ):
        proj = scratch[: 2 * chunks]
        turned_r, turned_i, corr_acc = scratch[2 * chunks : 2 * chunks + 3]
        base_cos, base_sin, step_cos, step_sin, far_r, far_i = scratch[
            2 * chunks + 3 : 2 * chunks + 9
        ]
        table_sem, own_sem = scratch[2 * chunks + 9 :]

        def table_copies(tile):
            pairs = (base_c, base_cos), (base_s, base_sin), (step_c, step_cos), (step_s, step_sin)
            return [
                pltpu.make_async_copy(
                    source.at[tile, pl.ds(0, mixed)], target.at[tile], table_sem.at[tile, i]
                )
                for i, (source, target) in enumerate(pairs)
            ]

        def own_copies(tile):
            return [
                pltpu.make_async_copy(source.at[tile], target.at[tile], own_sem.at[tile, i])
                for i, (source, target) in enumerate(((own_r, far_r), (own_i, far_i)))
            ]

        for tile in range(tiles):
            for copy in table_copies(tile) + own_copies(tile):
                copy.start()

        pieces = 2 * (pixels // piece)

        def project(tile, part, low, high):
            for index in range(low, high):
                first, half = (index // 2) * piece, index % 2
                proj[2 * part + half][:, pl.ds(first, piece)] = lax.dot_general(
                    rows_ref[pl.ds(part * chunk, chunk), pl.ds(half * bins, bins)],
                    weight_ref[class_ref[tile], pl.ds(first, piece), :],
                    (((1,), (1,)), ((), ())),
                    preferred_element_type=jnp.float32,
                )

        def turn(tile, part, sums):
            for group in range(chunk // 8):
                at = pl.ds(part * chunk + group * 8, 8)

                def put(ref, at=at):
                    def store(lanes, value):
                        ref[at, lanes] = value

                    return store

                sums = turn_rows(
                    proj[2 * part], proj[2 * part + 1], pl.ds(group * 8, 8),
                    base_cos[tile, at, :], base_sin[tile, at, :],
                    step_cos[tile, at, :], step_sin[tile, at, :],
                    put(turned_r), put(turned_i), sums,
                )
            return sums

        def one_tile(tile, _):
            sums = [jnp.zeros((8, LANES), jnp.float32)] * (2 * blocks)
            for copy in table_copies(tile):
                copy.wait()
            for part in range(chunks):
                last = part + 1 == chunks
                following = jnp.minimum(tile + 1, tiles - 1) if last else tile
                project(following, (part + 1) % chunks, 0, pieces)
                sums = turn(tile, part, sums)
            for copy in own_copies(tile):
                copy.wait()
            heavy = []
            for b in range(blocks):
                lanes = pl.ds(b * LANES, LANES)
                real = far_r[tile, own : own + 1, lanes] + jnp.sum(sums[2 * b], axis=0, keepdims=True)
                imag = far_i[tile, own : own + 1, lanes] + jnp.sum(sums[2 * b + 1], axis=0, keepdims=True)
                image_ref[tile, 0:1, lanes] = real
                image_ref[tile, 1:2, lanes] = imag
                intensity = real * real + imag * imag
                heavy.append(jnp.broadcast_to(intensity * real, (8, LANES)))
                heavy.append(jnp.broadcast_to(intensity * imag, (8, LANES)))
            for group in range((mixed + own) // 8):
                at = pl.ds(group * 8, 8)
                total = corr_acc[at, :]
                for b in range(blocks):
                    lanes = pl.ds(b * LANES, LANES)
                    if group * 8 < mixed:
                        real, imag = turned_r[at, lanes], turned_i[at, lanes]
                    else:
                        near = pl.ds(group * 8 - mixed, 8)
                        real, imag = far_r[tile, near, lanes], far_i[tile, near, lanes]
                    total = total + (real * heavy[2 * b + 1] - imag * heavy[2 * b])
                corr_acc[at, :] = total
            return 0

        corr_acc[...] = jnp.zeros_like(corr_acc)
        project(0, 0, 0, pieces)
        lax.fori_loop(0, tiles, one_tile, 0)
        totals = jnp.sum(corr_acc[...], axis=1, keepdims=True)
        row = lax.broadcasted_iota(jnp.int32, (mixed + own, LANES), 0)
        lane = lax.broadcasted_iota(jnp.int32, (mixed + own, LANES), 1)
        placed = jnp.where(row % cap == lane, totals, 0.0)
        placed = jnp.sum(placed.reshape((mixed + own) // cap, cap, LANES), axis=1)
        corr_acc[pl.ds(0, (mixed + own) // cap), :] = placed
        corr_ref[...] = jnp.zeros_like(corr_ref)
        track = track_ref[0]
        sources = own // cap
        cuts = (pl.ds(0, sources, stride=2), pl.ds(2 * sources, sources), pl.ds(1, sources, stride=2))
        for k, cut in enumerate(cuts):

            @pl.when((track + k >= 1) & (track + k <= tracks))
            def _(k=k, cut=cut):
                target = pl.ds(pl.multiple_of((track + k - 1) * sources, sources), sources)
                corr_ref[target, :] = corr_acc[cut, :][:, :cap]

    return focus_kernel


def focus(tile_class, track, arrived, weight_tiles, tables, own_parts, chunk, piece, tracks, cap):
    turned_own_r, turned_own_i = own_parts
    mixed, _ = arrived.shape
    own = turned_own_r.shape[1] - 8
    slots = mixed + own
    _, pixels, bins = weight_tiles.shape
    tiles = tile_class.shape[0]
    vmem = pl.BlockSpec(memory_space=pltpu.VMEM)
    hbm = pl.BlockSpec(memory_space=pltpu.HBM)
    image, corr = pl.pallas_call(
        make_focus_kernel(mixed, own, pixels, bins, tiles, chunk, piece, tracks, cap),
        in_specs=[pl.BlockSpec(memory_space=pltpu.SMEM)] * 2 + [vmem] * 2 + [hbm] * 6,
        out_specs=[vmem] * 2,
        scratch_shapes=[pltpu.VMEM((chunk, pixels), jnp.float32)] * (2 * (mixed // chunk))
        + [
            pltpu.VMEM((mixed, pixels), jnp.float32),
            pltpu.VMEM((mixed, pixels), jnp.float32),
            pltpu.VMEM((slots, LANES), jnp.float32),
        ]
        + [pltpu.VMEM((tiles, mixed, LANES), jnp.float32)] * 4
        + [pltpu.VMEM((tiles, own + 8, pixels), jnp.float32)] * 2
        + [
            pltpu.SemaphoreType.DMA((tiles, 4)),
            pltpu.SemaphoreType.DMA((tiles, 2)),
        ],
        out_shape=[
            jax.ShapeDtypeStruct((tiles, 2, pixels), jnp.float32),
            jax.ShapeDtypeStruct((tracks * own // cap, cap), jnp.float32),
        ],
        compiler_params=pltpu.CompilerParams(vmem_limit_bytes=52 * 1024 * 1024),
        name="focus",
    )(tile_class, track, arrived, weight_tiles, *tables, turned_own_r, turned_own_i)
    return image, corr


def on_device(
    panels, phases, weight_tiles, tile_class, send_slots, foot_slot, foot_ping, tile_counts
):
    track_devs = lax.axis_size("track")
    tile_devs = lax.axis_size("tile")
    device = lax.axis_index("track") * tile_devs + lax.axis_index("tile")
    ping_local = phases.shape[0]
    row_width = panels.shape[1]
    tiles_here = tile_counts.shape[0]
    pixels = weight_tiles.shape[1]
    slots = send_slots.shape[0]
    slot_cap = slots // 3 // tile_devs
    ping_total = ping_local * track_devs * tile_devs
    tile_total = tiles_here * track_devs * tile_devs

    blocks = (tile_devs, slot_cap, row_width)
    group = slots // 3
    to_next, to_last, own = gather_rotated(panels, phases, send_slots, (2, 0, 1))
    behind = shift_along(to_next.reshape(blocks), "track", 1)
    ahead = shift_along(to_last.reshape(blocks), "track", -1)
    own_arrived = lax.all_to_all(
        own.reshape(blocks), "tile", split_axis=0, concat_axis=0, tiled=True
    )
    mixed = jnp.concatenate([behind, ahead], axis=1)
    arrived = lax.all_to_all(mixed, "tile", split_axis=0, concat_axis=0, tiled=True)
    tables = phase_tables(
        (device * tiles_here).astype(jnp.int32).reshape(1),
        tile_counts, foot_slot, foot_ping, slots,
        ping_total, tile_total, track_devs, tile_devs, pixels,
    )
    own_parts = own_forward(
        tile_class, own_arrived.reshape(group, row_width), weight_tiles, tables, 2 * group
    )
    track = lax.axis_index("track")
    image, corr = focus(
        tile_class, track.astype(jnp.int32).reshape(1), arrived.reshape(2 * group, row_width),
        weight_tiles, tables, own_parts, group, 256, track_devs, slot_cap,
    )
    back = lax.all_to_all(corr, ("track", "tile"), split_axis=0, concat_axis=0, tiled=True)
    back = jnp.pad(back.reshape(track_devs, tile_devs, slot_cap), ((1, 1), (0, 0), (0, 0)))
    back = lax.dynamic_slice_in_dim(back, track, 3, 0).reshape(1, slots)
    owner = (send_slots // (panels.shape[0] // ping_local)).reshape(1, slots)
    mine = lax.broadcasted_iota(jnp.int32, (ping_local, slots), 0) == owner
    ping_gradient = jnp.sum(jnp.where(mine & (send_slots >= 0)[None, :], back, 0.0), axis=1)
    return (image, ping_gradient)


def solution(mesh):
    spread = P(("track", "tile"))
    in_specs = (
        P(("track", "tile"), None), spread, P(), spread, spread,
        P(("track", "tile"), None), P(("track", "tile"), None), spread,
    )
    out_specs = (P(("track", "tile"), None, None), spread)
    return jax.shard_map(
        on_device, mesh=mesh, in_specs=in_specs, out_specs=out_specs, check_vma=False
    )
```

```python
import functools
import math

import jax
import jax.numpy as jnp
from jax import lax
from jax.experimental import pallas as pl
from jax.experimental.pallas import tpu as pltpu
from jax.sharding import PartitionSpec as P

LANES = 128
HALF = 128
ALL_VMEM = 60 * 1024 * 1024


def shift_along(block, axis, distance):
    devices = range(lax.axis_size(axis))
    route = [(i - distance, i) for i in devices if i - distance in devices]
    return lax.ppermute(block, axis, route)


def whole(shape):
    return pl.BlockSpec(shape, lambda *_: (0,) * len(shape))


def column(row):
    return jnp.broadcast_to(row, (8, row.shape[1])).T[:, :1]


def rotated_rows(panels_ref, cosine, sine, slots_ref, first, count):
    rows_here, width = panels_ref.shape
    bins = width // 2
    pings = cosine.shape[1]
    columns = [
        column(slots_ref[pl.ds(row, 1), :].astype(jnp.float32))
        for row in range(first // LANES, (first + count) // LANES)
    ]
    slot_row = jnp.concatenate(columns, axis=0).astype(jnp.int32)
    row_ids = lax.broadcasted_iota(jnp.int32, (count, rows_here), 1)
    pick = jnp.where(row_ids == slot_row, 1.0, 0.0).astype(jnp.bfloat16)
    picked = jnp.dot(pick, panels_ref[...], preferred_element_type=jnp.float32)
    ping_ids = lax.broadcasted_iota(jnp.int32, (count, pings), 1)
    owned = ping_ids == (slot_row // (rows_here // pings))
    cos_col = jnp.sum(jnp.where(owned, cosine, 0.0), axis=1, keepdims=True)
    sin_col = jnp.sum(jnp.where(owned, sine, 0.0), axis=1, keepdims=True)
    real_part = picked[:, :bins]
    imag_part = picked[:, bins:]
    return (
        (cos_col * real_part - sin_col * imag_part).astype(jnp.bfloat16),
        (sin_col * real_part + cos_col * imag_part).astype(jnp.bfloat16),
    )


def gather_rotated(panels, phases, slots, offsets):
    count = slots.shape[0] // 3
    width = panels.shape[1]
    bins = width // 2

    def kernel(panels_ref, phases_ref, slots_ref, *outs):
        cosine, sine = cos_sin(phases_ref[...])
        for offset, out in zip(offsets, outs):
            real_part, imag_part = rotated_rows(
                panels_ref, cosine, sine, slots_ref, offset * count, count
            )
            out[:, :bins] = real_part
            out[:, bins:] = imag_part

    return pl.pallas_call(
        kernel,
        out_shape=[jax.ShapeDtypeStruct((count, width), jnp.bfloat16) for _ in offsets],
        compiler_params=pltpu.CompilerParams(vmem_limit_bytes=ALL_VMEM),
        name="gather_rotated",
    )(panels, phases.reshape(1, -1), slots.reshape(-1, LANES))


def cos_sin(angle):
    turns = jnp.round(angle * (2.0 / math.pi))
    rest = angle - turns * 1.5703125
    rest = rest - turns * 4.837512969970703125e-4
    rest = rest - turns * 7.549789948768648e-8
    square = rest * rest
    sine = (-1.9515295891e-4 * square + 8.3321608736e-3) * square - 1.6666654611e-1
    sine = sine * square * rest + rest
    cosine = (2.443315711809948e-5 * square - 1.388731625493765e-3) * square
    cosine = (cosine + 4.166664568298827e-2) * square * square - 0.5 * square + 1.0
    quarter = turns.astype(jnp.int32)
    odd = (quarter & 1) == 1
    cos_out = jnp.where(odd, sine, cosine)
    sin_out = jnp.where(odd, cosine, sine)
    cos_out = jnp.where(((quarter + 1) & 2) == 2, -cos_out, cos_out)
    sin_out = jnp.where((quarter & 2) == 2, -sin_out, sin_out)
    return cos_out, sin_out


def make_table_kernel(ping_total, tile_total, track_groups, pixels, tile_devs, slots, tiles):
    def table_kernel(base_ref, counts_ref, slot_ref, ping_ref, base_cos, base_sin, step_cos, step_sin):
        foot = slot_ref.shape[1]
        group = slots // 3
        cap = group // tile_devs
        slot_ids = lax.broadcasted_iota(jnp.int32, (slots, foot), 0)
        lane = lax.broadcasted_iota(jnp.int32, (1, LANES), 1)
        across = (lane.astype(jnp.float32) + 0.5) / pixels - 0.5
        step_angle = jnp.zeros((slots, LANES), jnp.float32)
        for tile in range(tiles):
            listed = slot_ref[tile : tile + 1, :]
            offset = listed // group
            source = (listed % group) // cap
            place = listed % cap
            placed = jnp.where(
                offset == 1,
                2 * group + source * cap + place,
                (source * 2 + offset // 2) * cap + place,
            )
            match = jnp.where(slot_ids == placed, 1.0, 0.0).astype(jnp.bfloat16)
            pings = ping_ref[tile : tile + 1, :]
            entry = lax.broadcasted_iota(jnp.int32, (1, foot), 1)
            used = jnp.where(entry < counts_ref[tile], 1.0, 0.0)
            values = jnp.concatenate(
                [
                    (pings // HALF).astype(jnp.float32) * used,
                    (pings % HALF).astype(jnp.float32) * used,
                    used,
                    jnp.zeros((5, foot), jnp.float32),
                ],
                axis=0,
            ).astype(jnp.bfloat16)
            found = lax.dot_general(
                match, values, (((1,), (1,)), ((), ())), preferred_element_type=jnp.float32
            )
            ping = (found[:, 0:1] * HALF + found[:, 1:2]).astype(jnp.int32)
            mask = found[:, 2:3]
            gap = (2 * ping + 1) * tile_total - (2 * (base_ref[0] + tile) + 1) * ping_total
            along = gap.astype(jnp.float32) * (track_groups / (2.0 * ping_total * tile_total))
            cosine, sine = cos_sin(96.0 * across * along + 8.0 * (along * along))
            base_cos[tile] = cosine * mask
            base_sin[tile] = sine * mask
            step_angle = jnp.where(lane == tile, (96.0 * LANES / pixels) * along, step_angle)
        cosine, sine = cos_sin(step_angle)
        for tile in range(tiles):
            step_cos[tile] = jnp.broadcast_to(cosine[:, tile : tile + 1], (slots, LANES))
            step_sin[tile] = jnp.broadcast_to(sine[:, tile : tile + 1], (slots, LANES))

    return table_kernel


def phase_tables(
    base, counts, foot_slot, foot_ping, slots, ping_total, tile_total, track_groups, tile_devs, pixels
):
    tiles, foot = foot_slot.shape
    kernel = make_table_kernel(ping_total, tile_total, track_groups, pixels, tile_devs, slots, tiles)
    table = jax.ShapeDtypeStruct((tiles, slots, LANES), jnp.float32)
    smem = pl.BlockSpec(memory_space=pltpu.SMEM)
    vmem = pl.BlockSpec(memory_space=pltpu.VMEM)
    return pl.pallas_call(
        kernel,
        in_specs=[smem, smem, vmem, vmem],
        out_specs=[vmem] * 4,
        out_shape=[table] * 4,
        compiler_params=pltpu.CompilerParams(vmem_limit_bytes=ALL_VMEM),
        name="phase_tables",
    )(base, counts, foot_slot, foot_ping)


def turn_rows(real_ref, imag_ref, rows, cos_now, sin_now, turn_c, turn_s, out_r, out_i, sums):
    blocks = len(sums) // 2
    sums = list(sums)
    for b in range(blocks):
        lanes = pl.ds(b * LANES, LANES)
        real = real_ref[rows, lanes]
        imag = imag_ref[rows, lanes]
        new_r = cos_now * real - sin_now * imag
        new_i = sin_now * real + cos_now * imag
        out_r(lanes, new_r)
        out_i(lanes, new_i)
        sums[2 * b] = sums[2 * b] + new_r
        sums[2 * b + 1] = sums[2 * b + 1] + new_i
        if b + 1 < blocks:
            cos_now, sin_now = (
                cos_now * turn_c - sin_now * turn_s,
                sin_now * turn_c + cos_now * turn_s,
            )
    return sums


def project_rows(rows_ref, first_row, count, weight, out_r, out_i, bins, pixels, piece):
    for first in range(0, pixels, piece):
        for half, out in enumerate((out_r, out_i)):
            out[:, pl.ds(first, piece)] = lax.dot_general(
                rows_ref[pl.ds(first_row, count), pl.ds(half * bins, bins)],
                weight(first, piece),
                (((1,), (1,)), ((), ())),
                preferred_element_type=jnp.float32,
            )


def own_forward(tile_class, own, weight_tiles, tables, first_slot):
    count, width = own.shape
    _, pixels, bins = weight_tiles.shape
    tiles = tile_class.shape[0]
    blocks = pixels // LANES
    block_at = first_slot // count

    def kernel(class_ref, rows_ref, weight_ref, base_c, base_s, step_c, step_s, turned_r, turned_i, proj_r, proj_i):
        project_rows(
            rows_ref, 0, count, lambda first, size: weight_ref[0, pl.ds(first, size), :],
            proj_r, proj_i, bins, pixels, pixels,
        )

        def group(i, sums):
            at = pl.ds(pl.multiple_of(i * 8, 8), 8)

            def put(ref):
                def store(lanes, value):
                    ref[0, at, lanes] = value

                return store

            return tuple(
                turn_rows(
                    proj_r, proj_i, at, base_c[0, at, :], base_s[0, at, :], step_c[0, at, :],
                    step_s[0, at, :], put(turned_r), put(turned_i), sums,
                )
            )

        sums = (jnp.zeros((8, LANES), jnp.float32),) * (2 * blocks)
        sums = lax.fori_loop(0, count // 8, group, sums, unroll=4)
        for b in range(blocks):
            for half in range(2):
                total = jnp.sum(sums[2 * b + half], axis=0, keepdims=True)
                store = turned_i if half else turned_r
                store[0, pl.ds(count, 8), pl.ds(b * LANES, LANES)] = jnp.broadcast_to(total, (8, LANES))

    table_spec = pl.BlockSpec((1, count, LANES), lambda t, *_: (t, block_at, 0))
    turned = jax.ShapeDtypeStruct((tiles, count + 8, pixels), jnp.float32)
    turned_spec = pl.BlockSpec((1, count + 8, pixels), lambda t, *_: (t, 0, 0))
    return pl.pallas_call(
        kernel,
        grid_spec=pltpu.PrefetchScalarGridSpec(
            num_scalar_prefetch=1,
            grid=(tiles,),
            in_specs=[
                pl.BlockSpec((count, width), lambda t, *_: (0, 0)),
                pl.BlockSpec((1, pixels, bins), lambda t, cls: (cls[t], 0, 0)),
            ]
            + [table_spec] * 4,
            out_specs=[turned_spec, turned_spec],
            scratch_shapes=[pltpu.VMEM((count, pixels), jnp.float32)] * 2,
        ),
        out_shape=[turned, turned],
        compiler_params=pltpu.CompilerParams(vmem_limit_bytes=ALL_VMEM),
        name="own_forward",
    )(tile_class, own, weight_tiles, *tables)


def make_focus_kernel(mixed, own, pixels, bins, tiles, chunk, piece, tracks, cap):
    blocks = pixels // LANES
    chunks = mixed // chunk

    def focus_kernel(
        class_ref, track_ref, rows_ref, weight_ref, base_c, base_s, step_c, step_s, own_r, own_i,
        image_ref, corr_ref, *scratch,
    ):
        proj = scratch[: 2 * chunks]
        turned_r, turned_i, corr_acc = scratch[2 * chunks : 2 * chunks + 3]
        base_cos, base_sin, step_cos, step_sin, far_r, far_i = scratch[
            2 * chunks + 3 : 2 * chunks + 9
        ]
        table_sem, own_sem = scratch[2 * chunks + 9 :]

        def table_copies(tile):
            pairs = (base_c, base_cos), (base_s, base_sin), (step_c, step_cos), (step_s, step_sin)
            return [
                pltpu.make_async_copy(
                    source.at[tile, pl.ds(0, mixed)], target.at[tile], table_sem.at[tile, i]
                )
                for i, (source, target) in enumerate(pairs)
            ]

        def own_copies(tile):
            return [
                pltpu.make_async_copy(source.at[tile], target.at[tile], own_sem.at[tile, i])
                for i, (source, target) in enumerate(((own_r, far_r), (own_i, far_i)))
            ]

        for tile in range(tiles):
            for copy in table_copies(tile) + own_copies(tile):
                copy.start()

        pieces = 2 * (pixels // piece)

        def project(tile, part, low, high):
            for index in range(low, high):
                first, half = (index // 2) * piece, index % 2
                proj[2 * part + half][:, pl.ds(first, piece)] = lax.dot_general(
                    rows_ref[pl.ds(part * chunk, chunk), pl.ds(half * bins, bins)],
                    weight_ref[class_ref[tile], pl.ds(first, piece), :],
                    (((1,), (1,)), ((), ())),
                    preferred_element_type=jnp.float32,
                )

        def turn(tile, part, sums):
            for group in range(chunk // 8):
                at = pl.ds(part * chunk + group * 8, 8)

                def put(ref, at=at):
                    def store(lanes, value):
                        ref[at, lanes] = value

                    return store

                sums = turn_rows(
                    proj[2 * part], proj[2 * part + 1], pl.ds(group * 8, 8),
                    base_cos[tile, at, :], base_sin[tile, at, :],
                    step_cos[tile, at, :], step_sin[tile, at, :],
                    put(turned_r), put(turned_i), sums,
                )
            return sums

        def one_tile(tile, _):
            sums = [jnp.zeros((8, LANES), jnp.float32)] * (2 * blocks)
            for copy in table_copies(tile):
                copy.wait()
            for part in range(chunks):
                last = part + 1 == chunks
                following = jnp.minimum(tile + 1, tiles - 1) if last else tile
                project(following, (part + 1) % chunks, 0, pieces)
                sums = turn(tile, part, sums)
            for copy in own_copies(tile):
                copy.wait()
            heavy = []
            for b in range(blocks):
                lanes = pl.ds(b * LANES, LANES)
                real = far_r[tile, own : own + 1, lanes] + jnp.sum(sums[2 * b], axis=0, keepdims=True)
                imag = far_i[tile, own : own + 1, lanes] + jnp.sum(sums[2 * b + 1], axis=0, keepdims=True)
                image_ref[tile, 0:1, lanes] = real
                image_ref[tile, 1:2, lanes] = imag
                intensity = real * real + imag * imag
                heavy.append(jnp.broadcast_to(intensity * real, (8, LANES)))
                heavy.append(jnp.broadcast_to(intensity * imag, (8, LANES)))
            for group in range((mixed + own) // 8):
                at = pl.ds(group * 8, 8)
                total = corr_acc[at, :]
                for b in range(blocks):
                    lanes = pl.ds(b * LANES, LANES)
                    if group * 8 < mixed:
                        real, imag = turned_r[at, lanes], turned_i[at, lanes]
                    else:
                        near = pl.ds(group * 8 - mixed, 8)
                        real, imag = far_r[tile, near, lanes], far_i[tile, near, lanes]
                    total = total + (real * heavy[2 * b + 1] - imag * heavy[2 * b])
                corr_acc[at, :] = total
            return 0

        corr_acc[...] = jnp.zeros_like(corr_acc)
        project(0, 0, 0, pieces)
        lax.fori_loop(0, tiles, one_tile, 0)
        corr_ref[...] = jnp.zeros_like(corr_ref)
        lane = lax.broadcasted_iota(jnp.int32, (cap, LANES), 1)
        pick = lax.broadcasted_iota(jnp.int32, (cap, LANES), 0) == lane
        track = track_ref[0]
        sources = own // cap
        placed = []
        for source in range((mixed + own) // cap):
            total = jnp.sum(corr_acc[pl.ds(source * cap, cap), :], axis=1, keepdims=True)
            placed.append(jnp.sum(jnp.where(pick, total, 0.0), axis=0, keepdims=True))
        starts = (placed[0 : 2 * sources : 2], placed[2 * sources :], placed[1 : 2 * sources : 2])
        for k, part in enumerate(starts):
            block = jnp.concatenate(part, axis=0)[:, :cap]

            @pl.when((track + k >= 1) & (track + k <= tracks))
            def _(k=k, block=block):
                target = pl.ds(pl.multiple_of((track + k - 1) * sources, sources), sources)
                corr_ref[target, :] = block

    return focus_kernel


def focus(tile_class, track, arrived, weight_tiles, tables, own_parts, chunk, piece, tracks, cap):
    turned_own_r, turned_own_i = own_parts
    mixed, _ = arrived.shape
    own = turned_own_r.shape[1] - 8
    slots = mixed + own
    _, pixels, bins = weight_tiles.shape
    tiles = tile_class.shape[0]
    vmem = pl.BlockSpec(memory_space=pltpu.VMEM)
    hbm = pl.BlockSpec(memory_space=pltpu.HBM)
    image, corr = pl.pallas_call(
        make_focus_kernel(mixed, own, pixels, bins, tiles, chunk, piece, tracks, cap),
        in_specs=[pl.BlockSpec(memory_space=pltpu.SMEM)] * 2 + [vmem] * 2 + [hbm] * 6,
        out_specs=[vmem] * 2,
        scratch_shapes=[pltpu.VMEM((chunk, pixels), jnp.float32)] * (2 * (mixed // chunk))
        + [
            pltpu.VMEM((mixed, pixels), jnp.float32),
            pltpu.VMEM((mixed, pixels), jnp.float32),
            pltpu.VMEM((slots, LANES), jnp.float32),
        ]
        + [pltpu.VMEM((tiles, mixed, LANES), jnp.float32)] * 4
        + [pltpu.VMEM((tiles, own + 8, pixels), jnp.float32)] * 2
        + [
            pltpu.SemaphoreType.DMA((tiles, 4)),
            pltpu.SemaphoreType.DMA((tiles, 2)),
        ],
        out_shape=[
            jax.ShapeDtypeStruct((tiles, 2, pixels), jnp.float32),
            jax.ShapeDtypeStruct((tracks * own // cap, cap), jnp.float32),
        ],
        compiler_params=pltpu.CompilerParams(vmem_limit_bytes=52 * 1024 * 1024),
        name="focus",
    )(tile_class, track, arrived, weight_tiles, *tables, turned_own_r, turned_own_i)
    return image, corr


def on_device(
    panels, phases, weight_tiles, tile_class, send_slots, foot_slot, foot_ping, tile_counts
):
    track_devs = lax.axis_size("track")
    tile_devs = lax.axis_size("tile")
    device = lax.axis_index("track") * tile_devs + lax.axis_index("tile")
    ping_local = phases.shape[0]
    row_width = panels.shape[1]
    tiles_here = tile_counts.shape[0]
    pixels = weight_tiles.shape[1]
    slots = send_slots.shape[0]
    slot_cap = slots // 3 // tile_devs
    ping_total = ping_local * track_devs * tile_devs
    tile_total = tiles_here * track_devs * tile_devs

    blocks = (tile_devs, slot_cap, row_width)
    group = slots // 3
    to_next, to_last, own = gather_rotated(panels, phases, send_slots, (2, 0, 1))
    behind = shift_along(to_next.reshape(blocks), "track", 1)
    ahead = shift_along(to_last.reshape(blocks), "track", -1)
    own_arrived = lax.all_to_all(
        own.reshape(blocks), "tile", split_axis=0, concat_axis=0, tiled=True
    )
    mixed = jnp.concatenate([behind, ahead], axis=1)
    arrived = lax.all_to_all(mixed, "tile", split_axis=0, concat_axis=0, tiled=True)
    tables = phase_tables(
        (device * tiles_here).astype(jnp.int32).reshape(1),
        tile_counts, foot_slot, foot_ping, slots,
        ping_total, tile_total, track_devs, tile_devs, pixels,
    )
    own_parts = own_forward(
        tile_class, own_arrived.reshape(group, row_width), weight_tiles, tables, 2 * group
    )
    track = lax.axis_index("track")
    image, corr = focus(
        tile_class, track.astype(jnp.int32).reshape(1), arrived.reshape(2 * group, row_width),
        weight_tiles, tables, own_parts, group, 256, track_devs, slot_cap,
    )
    back = lax.all_to_all(corr, ("track", "tile"), split_axis=0, concat_axis=0, tiled=True)
    back = jnp.pad(back.reshape(track_devs, tile_devs, slot_cap), ((1, 1), (0, 0), (0, 0)))
    back = lax.dynamic_slice_in_dim(back, track, 3, 0).reshape(1, slots)
    owner = (send_slots // (panels.shape[0] // ping_local)).reshape(1, slots)
    mine = lax.broadcasted_iota(jnp.int32, (ping_local, slots), 0) == owner
    ping_gradient = jnp.sum(jnp.where(mine & (send_slots >= 0)[None, :], back, 0.0), axis=1)
    return (image, ping_gradient)


def solution(mesh):
    spread = P(("track", "tile"))
    in_specs = (
        P(("track", "tile"), None), spread, P(), spread, spread,
        P(("track", "tile"), None), P(("track", "tile"), None), spread,
    )
    out_specs = (P(("track", "tile"), None, None), spread)
    return jax.shard_map(
        on_device, mesh=mesh, in_specs=in_specs, out_specs=out_specs, check_vma=False
    )
```

```python
import functools
import math

import jax
import jax.numpy as jnp
from jax import lax
from jax.experimental import pallas as pl
from jax.experimental.pallas import tpu as pltpu
from jax.sharding import PartitionSpec as P

LANES = 128
HALF = 128
ALL_VMEM = 60 * 1024 * 1024


def shift_along(block, axis, distance):
    devices = range(lax.axis_size(axis))
    route = [(i - distance, i) for i in devices if i - distance in devices]
    return lax.ppermute(block, axis, route)


def whole(shape):
    return pl.BlockSpec(shape, lambda *_: (0,) * len(shape))


def column(row):
    return jnp.broadcast_to(row, (8, row.shape[1])).T[:, :1]


def rotated_rows(panels_ref, phases_ref, slots_ref, first, count):
    rows_here, width = panels_ref.shape
    bins = width // 2
    pings = phases_ref.shape[1]
    columns = [
        column(slots_ref[pl.ds(row, 1), :].astype(jnp.float32))
        for row in range(first // LANES, (first + count) // LANES)
    ]
    slot_row = jnp.concatenate(columns, axis=0).astype(jnp.int32)
    row_ids = lax.broadcasted_iota(jnp.int32, (count, rows_here), 1)
    pick = jnp.where(row_ids == slot_row, 1.0, 0.0).astype(jnp.bfloat16)
    picked = jnp.dot(pick, panels_ref[...], preferred_element_type=jnp.float32)
    phases = phases_ref[...]
    ping_ids = lax.broadcasted_iota(jnp.int32, (count, pings), 1)
    owned = ping_ids == (slot_row // (rows_here // pings))
    cos_col = jnp.sum(jnp.where(owned, jnp.cos(phases), 0.0), axis=1, keepdims=True)
    sin_col = jnp.sum(jnp.where(owned, jnp.sin(phases), 0.0), axis=1, keepdims=True)
    real_part = picked[:, :bins]
    imag_part = picked[:, bins:]
    return (
        (cos_col * real_part - sin_col * imag_part).astype(jnp.bfloat16),
        (sin_col * real_part + cos_col * imag_part).astype(jnp.bfloat16),
    )


def gather_rotated(panels, phases, slots, offsets):
    count = slots.shape[0] // 3
    width = panels.shape[1]
    bins = width // 2

    def kernel(panels_ref, phases_ref, slots_ref, *outs):
        for offset, out in zip(offsets, outs):
            real_part, imag_part = rotated_rows(
                panels_ref, phases_ref, slots_ref, offset * count, count
            )
            out[:, :bins] = real_part
            out[:, bins:] = imag_part

    return pl.pallas_call(
        kernel,
        out_shape=[jax.ShapeDtypeStruct((count, width), jnp.bfloat16) for _ in offsets],
        compiler_params=pltpu.CompilerParams(vmem_limit_bytes=24 * 1024 * 1024),
        name="gather_rotated",
    )(panels, phases.reshape(1, -1), slots.reshape(-1, LANES))


def cos_sin(angle):
    turns = jnp.round(angle * (2.0 / math.pi))
    rest = angle - turns * 1.5703125
    rest = rest - turns * 4.837512969970703125e-4
    rest = rest - turns * 7.549789948768648e-8
    square = rest * rest
    sine = (-1.9515295891e-4 * square + 8.3321608736e-3) * square - 1.6666654611e-1
    sine = sine * square * rest + rest
    cosine = (2.443315711809948e-5 * square - 1.388731625493765e-3) * square
    cosine = (cosine + 4.166664568298827e-2) * square * square - 0.5 * square + 1.0
    quarter = turns.astype(jnp.int32)
    odd = (quarter & 1) == 1
    cos_out = jnp.where(odd, sine, cosine)
    sin_out = jnp.where(odd, cosine, sine)
    cos_out = jnp.where(((quarter + 1) & 2) == 2, -cos_out, cos_out)
    sin_out = jnp.where((quarter & 2) == 2, -sin_out, sin_out)
    return cos_out, sin_out


def make_table_kernel(ping_total, tile_total, track_groups, pixels, tile_devs, slots, tiles):
    def table_kernel(base_ref, counts_ref, slot_ref, ping_ref, base_cos, base_sin, step_cos, step_sin):
        foot = slot_ref.shape[1]
        group = slots // 3
        cap = group // tile_devs
        slot_ids = lax.broadcasted_iota(jnp.int32, (slots, foot), 0)
        lane = lax.broadcasted_iota(jnp.int32, (1, LANES), 1)
        across = (lane.astype(jnp.float32) + 0.5) / pixels - 0.5
        step_angle = jnp.zeros((slots, LANES), jnp.float32)
        for tile in range(tiles):
            listed = slot_ref[tile : tile + 1, :]
            offset = listed // group
            source = (listed % group) // cap
            place = listed % cap
            placed = jnp.where(
                offset == 1,
                2 * group + source * cap + place,
                (source * 2 + offset // 2) * cap + place,
            )
            match = jnp.where(slot_ids == placed, 1.0, 0.0).astype(jnp.bfloat16)
            pings = ping_ref[tile : tile + 1, :]
            entry = lax.broadcasted_iota(jnp.int32, (1, foot), 1)
            used = jnp.where(entry < counts_ref[tile], 1.0, 0.0)
            values = jnp.concatenate(
                [
                    (pings // HALF).astype(jnp.float32) * used,
                    (pings % HALF).astype(jnp.float32) * used,
                    used,
                    jnp.zeros((5, foot), jnp.float32),
                ],
                axis=0,
            ).astype(jnp.bfloat16)
            found = lax.dot_general(
                match, values, (((1,), (1,)), ((), ())), preferred_element_type=jnp.float32
            )
            ping = (found[:, 0:1] * HALF + found[:, 1:2]).astype(jnp.int32)
            mask = found[:, 2:3]
            gap = (2 * ping + 1) * tile_total - (2 * (base_ref[0] + tile) + 1) * ping_total
            along = gap.astype(jnp.float32) * (track_groups / (2.0 * ping_total * tile_total))
            cosine, sine = cos_sin(96.0 * across * along + 8.0 * (along * along))
            base_cos[tile] = cosine * mask
            base_sin[tile] = sine * mask
            step_angle = jnp.where(lane == tile, (96.0 * LANES / pixels) * along, step_angle)
        cosine, sine = cos_sin(step_angle)
        for tile in range(tiles):
            step_cos[tile] = jnp.broadcast_to(cosine[:, tile : tile + 1], (slots, LANES))
            step_sin[tile] = jnp.broadcast_to(sine[:, tile : tile + 1], (slots, LANES))

    return table_kernel


def phase_tables(
    base, counts, foot_slot, foot_ping, slots, ping_total, tile_total, track_groups, tile_devs, pixels
):
    tiles, foot = foot_slot.shape
    kernel = make_table_kernel(ping_total, tile_total, track_groups, pixels, tile_devs, slots, tiles)
    table = jax.ShapeDtypeStruct((tiles, slots, LANES), jnp.float32)
    smem = pl.BlockSpec(memory_space=pltpu.SMEM)
    vmem = pl.BlockSpec(memory_space=pltpu.VMEM)
    return pl.pallas_call(
        kernel,
        in_specs=[smem, smem, vmem, vmem],
        out_specs=[vmem] * 4,
        out_shape=[table] * 4,
        compiler_params=pltpu.CompilerParams(vmem_limit_bytes=ALL_VMEM),
        name="phase_tables",
    )(base, counts, foot_slot, foot_ping)


def turn_rows(real_ref, imag_ref, rows, cos_now, sin_now, turn_c, turn_s, out_r, out_i, sums):
    blocks = len(sums) // 2
    sums = list(sums)
    for b in range(blocks):
        lanes = pl.ds(b * LANES, LANES)
        real = real_ref[rows, lanes]
        imag = imag_ref[rows, lanes]
        new_r = cos_now * real - sin_now * imag
        new_i = sin_now * real + cos_now * imag
        out_r(lanes, new_r)
        out_i(lanes, new_i)
        sums[2 * b] = sums[2 * b] + new_r
        sums[2 * b + 1] = sums[2 * b + 1] + new_i
        if b + 1 < blocks:
            cos_now, sin_now = (
                cos_now * turn_c - sin_now * turn_s,
                sin_now * turn_c + cos_now * turn_s,
            )
    return sums


def project_rows(rows_ref, first_row, count, weight, out_r, out_i, bins, pixels, piece):
    for first in range(0, pixels, piece):
        for half, out in enumerate((out_r, out_i)):
            out[:, pl.ds(first, piece)] = lax.dot_general(
                rows_ref[pl.ds(first_row, count), pl.ds(half * bins, bins)],
                weight(first, piece),
                (((1,), (1,)), ((), ())),
                preferred_element_type=jnp.float32,
            )


def own_forward(tile_class, own, weight_tiles, tables, first_slot):
    count, width = own.shape
    _, pixels, bins = weight_tiles.shape
    tiles = tile_class.shape[0]
    blocks = pixels // LANES
    block_at = first_slot // count

    def kernel(class_ref, rows_ref, weight_ref, base_c, base_s, step_c, step_s, turned_r, turned_i, proj_r, proj_i):
        project_rows(
            rows_ref, 0, count, lambda first, size: weight_ref[0, pl.ds(first, size), :],
            proj_r, proj_i, bins, pixels, pixels,
        )

        def group(i, sums):
            at = pl.ds(pl.multiple_of(i * 8, 8), 8)

            def put(ref):
                def store(lanes, value):
                    ref[0, at, lanes] = value

                return store

            return tuple(
                turn_rows(
                    proj_r, proj_i, at, base_c[0, at, :], base_s[0, at, :], step_c[0, at, :],
                    step_s[0, at, :], put(turned_r), put(turned_i), sums,
                )
            )

        sums = (jnp.zeros((8, LANES), jnp.float32),) * (2 * blocks)
        sums = lax.fori_loop(0, count // 8, group, sums, unroll=4)
        for b in range(blocks):
            for half in range(2):
                total = jnp.sum(sums[2 * b + half], axis=0, keepdims=True)
                store = turned_i if half else turned_r
                store[0, pl.ds(count, 8), pl.ds(b * LANES, LANES)] = jnp.broadcast_to(total, (8, LANES))

    table_spec = pl.BlockSpec((1, count, LANES), lambda t, *_: (t, block_at, 0))
    turned = jax.ShapeDtypeStruct((tiles, count + 8, pixels), jnp.float32)
    turned_spec = pl.BlockSpec((1, count + 8, pixels), lambda t, *_: (t, 0, 0))
    return pl.pallas_call(
        kernel,
        grid_spec=pltpu.PrefetchScalarGridSpec(
            num_scalar_prefetch=1,
            grid=(tiles,),
            in_specs=[
                pl.BlockSpec((count, width), lambda t, *_: (0, 0)),
                pl.BlockSpec((1, pixels, bins), lambda t, cls: (cls[t], 0, 0)),
            ]
            + [table_spec] * 4,
            out_specs=[turned_spec, turned_spec],
            scratch_shapes=[pltpu.VMEM((count, pixels), jnp.float32)] * 2,
        ),
        out_shape=[turned, turned],
        compiler_params=pltpu.CompilerParams(vmem_limit_bytes=ALL_VMEM),
        name="own_forward",
    )(tile_class, own, weight_tiles, *tables)


def make_focus_kernel(mixed, own, pixels, bins, tiles, chunk, piece, tracks, cap):
    blocks = pixels // LANES
    chunks = mixed // chunk

    def focus_kernel(
        class_ref, track_ref, rows_ref, weight_ref, base_c, base_s, step_c, step_s, own_r, own_i,
        image_ref, corr_ref, *scratch,
    ):
        proj = scratch[: 2 * chunks]
        turned_r, turned_i, corr_acc = scratch[2 * chunks : 2 * chunks + 3]
        base_cos, base_sin, step_cos, step_sin, far_r, far_i = scratch[
            2 * chunks + 3 : 2 * chunks + 9
        ]
        table_sem, own_sem = scratch[2 * chunks + 9 :]

        def table_copies(tile):
            pairs = (base_c, base_cos), (base_s, base_sin), (step_c, step_cos), (step_s, step_sin)
            return [
                pltpu.make_async_copy(
                    source.at[tile, pl.ds(0, mixed)], target.at[tile], table_sem.at[tile, i]
                )
                for i, (source, target) in enumerate(pairs)
            ]

        def own_copies(tile):
            return [
                pltpu.make_async_copy(source.at[tile], target.at[tile], own_sem.at[tile, i])
                for i, (source, target) in enumerate(((own_r, far_r), (own_i, far_i)))
            ]

        for tile in range(tiles):
            for copy in table_copies(tile) + own_copies(tile):
                copy.start()

        pieces = 2 * (pixels // piece)

        def project(tile, part, low, high):
            for index in range(low, high):
                first, half = (index // 2) * piece, index % 2
                proj[2 * part + half][:, pl.ds(first, piece)] = lax.dot_general(
                    rows_ref[pl.ds(part * chunk, chunk), pl.ds(half * bins, bins)],
                    weight_ref[class_ref[tile], pl.ds(first, piece), :],
                    (((1,), (1,)), ((), ())),
                    preferred_element_type=jnp.float32,
                )

        def turn(tile, part, sums):
            for group in range(chunk // 8):
                at = pl.ds(part * chunk + group * 8, 8)

                def put(ref, at=at):
                    def store(lanes, value):
                        ref[at, lanes] = value

                    return store

                sums = turn_rows(
                    proj[2 * part], proj[2 * part + 1], pl.ds(group * 8, 8),
                    base_cos[tile, at, :], base_sin[tile, at, :],
                    step_cos[tile, at, :], step_sin[tile, at, :],
                    put(turned_r), put(turned_i), sums,
                )
            return sums

        def one_tile(tile, _):
            sums = [jnp.zeros((8, LANES), jnp.float32)] * (2 * blocks)
            for copy in table_copies(tile):
                copy.wait()
            for part in range(chunks):
                last = part + 1 == chunks
                following = jnp.minimum(tile + 1, tiles - 1) if last else tile
                project(following, (part + 1) % chunks, 0, pieces)
                sums = turn(tile, part, sums)
            for copy in own_copies(tile):
                copy.wait()
            heavy = []
            for b in range(blocks):
                lanes = pl.ds(b * LANES, LANES)
                real = far_r[tile, own : own + 1, lanes] + jnp.sum(sums[2 * b], axis=0, keepdims=True)
                imag = far_i[tile, own : own + 1, lanes] + jnp.sum(sums[2 * b + 1], axis=0, keepdims=True)
                image_ref[tile, 0:1, lanes] = real
                image_ref[tile, 1:2, lanes] = imag
                intensity = real * real + imag * imag
                heavy.append(jnp.broadcast_to(intensity * real, (8, LANES)))
                heavy.append(jnp.broadcast_to(intensity * imag, (8, LANES)))
            for group in range((mixed + own) // 8):
                at = pl.ds(group * 8, 8)
                total = corr_acc[at, :]
                for b in range(blocks):
                    lanes = pl.ds(b * LANES, LANES)
                    if group * 8 < mixed:
                        real, imag = turned_r[at, lanes], turned_i[at, lanes]
                    else:
                        near = pl.ds(group * 8 - mixed, 8)
                        real, imag = far_r[tile, near, lanes], far_i[tile, near, lanes]
                    total = total + (real * heavy[2 * b + 1] - imag * heavy[2 * b])
                corr_acc[at, :] = total
            return 0

        corr_acc[...] = jnp.zeros_like(corr_acc)
        project(0, 0, 0, pieces)
        lax.fori_loop(0, tiles, one_tile, 0)
        totals = jnp.sum(corr_acc[...], axis=1, keepdims=True)
        row = lax.broadcasted_iota(jnp.int32, (mixed + own, LANES), 0)
        lane = lax.broadcasted_iota(jnp.int32, (mixed + own, LANES), 1)
        placed = jnp.where(row % cap == lane, totals, 0.0)
        placed = jnp.sum(placed.reshape((mixed + own) // cap, cap, LANES), axis=1)
        corr_acc[pl.ds(0, (mixed + own) // cap), :] = placed
        corr_ref[...] = jnp.zeros_like(corr_ref)
        track = track_ref[0]
        sources = own // cap
        cuts = (pl.ds(0, sources, stride=2), pl.ds(2 * sources, sources), pl.ds(1, sources, stride=2))
        for k, cut in enumerate(cuts):

            @pl.when((track + k >= 1) & (track + k <= tracks))
            def _(k=k, cut=cut):
                target = pl.ds(pl.multiple_of((track + k - 1) * sources, sources), sources)
                corr_ref[target, :] = corr_acc[cut, :][:, :cap]

    return focus_kernel


def focus(tile_class, track, arrived, weight_tiles, tables, own_parts, chunk, piece, tracks, cap):
    turned_own_r, turned_own_i = own_parts
    mixed, _ = arrived.shape
    own = turned_own_r.shape[1] - 8
    slots = mixed + own
    _, pixels, bins = weight_tiles.shape
    tiles = tile_class.shape[0]
    vmem = pl.BlockSpec(memory_space=pltpu.VMEM)
    hbm = pl.BlockSpec(memory_space=pltpu.HBM)
    image, corr = pl.pallas_call(
        make_focus_kernel(mixed, own, pixels, bins, tiles, chunk, piece, tracks, cap),
        in_specs=[pl.BlockSpec(memory_space=pltpu.SMEM)] * 2 + [vmem] * 2 + [hbm] * 6,
        out_specs=[vmem] * 2,
        scratch_shapes=[pltpu.VMEM((chunk, pixels), jnp.float32)] * (2 * (mixed // chunk))
        + [
            pltpu.VMEM((mixed, pixels), jnp.float32),
            pltpu.VMEM((mixed, pixels), jnp.float32),
            pltpu.VMEM((slots, LANES), jnp.float32),
        ]
        + [pltpu.VMEM((tiles, mixed, LANES), jnp.float32)] * 4
        + [pltpu.VMEM((tiles, own + 8, pixels), jnp.float32)] * 2
        + [
            pltpu.SemaphoreType.DMA((tiles, 4)),
            pltpu.SemaphoreType.DMA((tiles, 2)),
        ],
        out_shape=[
            jax.ShapeDtypeStruct((tiles, 2, pixels), jnp.float32),
            jax.ShapeDtypeStruct((tracks * own // cap, cap), jnp.float32),
        ],
        compiler_params=pltpu.CompilerParams(vmem_limit_bytes=52 * 1024 * 1024),
        name="focus",
    )(tile_class, track, arrived, weight_tiles, *tables, turned_own_r, turned_own_i)
    return image, corr


def on_device(
    panels, phases, weight_tiles, tile_class, send_slots, foot_slot, foot_ping, tile_counts
):
    track_devs = lax.axis_size("track")
    tile_devs = lax.axis_size("tile")
    device = lax.axis_index("track") * tile_devs + lax.axis_index("tile")
    ping_local = phases.shape[0]
    row_width = panels.shape[1]
    tiles_here = tile_counts.shape[0]
    pixels = weight_tiles.shape[1]
    slots = send_slots.shape[0]
    slot_cap = slots // 3 // tile_devs
    ping_total = ping_local * track_devs * tile_devs
    tile_total = tiles_here * track_devs * tile_devs

    blocks = (tile_devs, slot_cap, row_width)
    group = slots // 3
    to_next, to_last, own = gather_rotated(panels, phases, send_slots, (2, 0, 1))
    behind = shift_along(to_next.reshape(blocks), "track", 1)
    ahead = shift_along(to_last.reshape(blocks), "track", -1)
    own_arrived = lax.all_to_all(
        own.reshape(blocks), "tile", split_axis=0, concat_axis=0, tiled=True
    )
    mixed = jnp.concatenate([behind, ahead], axis=1)
    arrived = lax.all_to_all(mixed, "tile", split_axis=0, concat_axis=0, tiled=True)
    tables = phase_tables(
        (device * tiles_here).astype(jnp.int32).reshape(1),
        tile_counts, foot_slot, foot_ping, slots,
        ping_total, tile_total, track_devs, tile_devs, pixels,
    )
    own_parts = own_forward(
        tile_class, own_arrived.reshape(group, row_width), weight_tiles, tables, 2 * group
    )
    track = lax.axis_index("track")
    image, corr = focus(
        tile_class, track.astype(jnp.int32).reshape(1), arrived.reshape(2 * group, row_width),
        weight_tiles, tables, own_parts, group, 256, track_devs, slot_cap,
    )
    back = lax.all_to_all(corr, ("track", "tile"), split_axis=0, concat_axis=0, tiled=True)
    back = jnp.pad(back.reshape(track_devs, tile_devs, slot_cap), ((1, 1), (0, 0), (0, 0)))
    back = lax.dynamic_slice_in_dim(back, track, 3, 0).reshape(1, slots)
    owner = (send_slots // (panels.shape[0] // ping_local)).reshape(1, slots)
    mine = lax.broadcasted_iota(jnp.int32, (ping_local, slots), 0) == owner
    ping_gradient = jnp.sum(jnp.where(mine & (send_slots >= 0)[None, :], back, 0.0), axis=1)
    return (image, ping_gradient)


def solution(mesh):
    spread = P(("track", "tile"))
    in_specs = (
        P(("track", "tile"), None), spread, P(), spread, spread,
        P(("track", "tile"), None), P(("track", "tile"), None), spread,
    )
    out_specs = (P(("track", "tile"), None, None), spread)
    return jax.shard_map(
        on_device, mesh=mesh, in_specs=in_specs, out_specs=out_specs, check_vma=False
    )
```
